512 devices in a mesh: tm: 64 (over z, y), rhs: 8 (over x, core).
Axes of the slice: x: 4, y: 8, z: 8, core: 2. Of those that a mesh axis runs over, the one named last changes fastest.
Arguments:
- jacobians: bfloat16 [128, 256, 256], P('tm', 'rhs'), may hold values from -0.065625 to 0.065625, as said below
- damping: float32 [128, 256], P('tm'), may hold values from 0.003 to 0.008
- right_sides: float32 [64, 128, 256], P('rhs', 'tm'), may hold values from -0.8 to 0.8, as said below
Outputs:
- solution: float32 [64, 128, 256], P('rhs', 'tm')
The draws below stay inside these ranges and needn't reach their ends.
Inputs may be any that keep to these rules, and one draw needn't show every extreme that they name: `jacobians`: real values of both signs. `right_sides`: real values, rough from section to section.
All inputs are finite; a program needn't handle non-finite values.
Results may differ from the reference program's by a relative error of at most 0.0003.
Values may be sent and summed in bfloat16 or wider, within the bound.
A program may use at most 128 MiB of HBM per device.

```python
import math
import jax
import jax.numpy as jnp
from jax import lax

NS = 256
SECTIONS = 128
RHS = 64


def column_shuffle(subkey):
    return jax.random.permutation(subkey, NS)


def draw_jacobians(key, part):
    subkeys = jax.random.split(key, 4)
    row_sign = (2 * jax.random.randint(subkeys[0], (SECTIONS, NS, 1), 0, 2) - 1).astype(jnp.float32)
    col_sign = (2 * jax.random.randint(subkeys[1], (SECTIONS, 1, NS), 0, 2) - 1).astype(jnp.float32)
    column_order = jax.vmap(column_shuffle)(jax.random.split(subkeys[2], SECTIONS)).astype(jnp.int32)
    row_ids = jnp.arange(NS, dtype=jnp.int32)[None, :, None]
    common = jnp.bitwise_and(row_ids, column_order[:, None, :])
    parity = jnp.zeros_like(common)
    for bit_index in range(NS.bit_length()):
        parity = jnp.bitwise_xor(parity, jnp.bitwise_and(jnp.right_shift(common, bit_index), 1))
    pattern = (1 - 2 * parity).astype(jnp.float32) * row_sign * col_sign
    spread = jax.random.uniform(subkeys[3], (SECTIONS, NS, NS), jnp.float32, -0.05, 0.05)
    magnitude = 0.99
    return (magnitude * NS ** (-0.5) * pattern * (1.0 + spread)).astype(jnp.bfloat16)


def draw_right_sides(key, part):
    values = 0.2 * jax.random.normal(key, (RHS, SECTIONS, NS), jnp.float32)
    return jnp.clip(values, -0.8, 0.8)


def shard_levels(key, dims, shards, smallest, largest):
    loudness, own = 1.0, jax.random.fold_in(key, 6)
    for position, shards_of in shards:
        heights = jnp.exp(jax.random.uniform(jax.random.fold_in(own, position), (shards_of,), jnp.float32, smallest / len(shards), largest / len(shards)))
        loudness = loudness * jnp.repeat(heights, dims[position] // shards_of).reshape([-1 if axis == position else 1 for axis in range(len(dims))])
    return loudness


def setup_inputs(seed: int = 0) -> dict:
    streams_of = jax.random.split(jax.random.key(seed), 4)
    return {
        "jacobians": draw_jacobians(jax.random.fold_in(streams_of[3], 71), 0),
        "damping": jnp.clip(jnp.exp(math.log(0.008) - 0.9808293 * jax.random.uniform(streams_of[1], (SECTIONS, NS), jnp.float32) ** shard_levels(streams_of[1], (SECTIONS, NS), ((0, 64),), -0.2, 0.2)), 0.003, 0.008),
        "right_sides": draw_right_sides(jax.random.fold_in(streams_of[3], 71), 0),
    }


HIGHEST = lax.Precision.HIGHEST

def lower_solve(factor, values):
    return lax.linalg.triangular_solve(factor, values, left_side=True, lower=True)

def upper_solve(factor, values):
    return lax.linalg.triangular_solve(factor, values, left_side=True, lower=True, transpose_a=True)

def tproduct(former, latter):
    return jnp.dot(former.T.astype(jnp.float32), latter.astype(jnp.float32), precision=HIGHEST, preferred_element_type=jnp.float32)

def reference(jacobians, damping, right_sides):
    identity = jnp.eye(NS, dtype=jnp.float32)
    section_ids = jnp.arange(SECTIONS, dtype=jnp.int32)
    columns = jnp.transpose(right_sides, (1, 2, 0))

    def coupling_of(jac_block, section_index):
        link_mask = jnp.where(section_index < SECTIONS - 1, 1.0, 0.0).astype(jnp.float32)
        return -jac_block.T.astype(jnp.float32) * link_mask

    def forward(running, section_item):
        link_prev, solved_prev = running
        jac_block, damp_row, column, section_index = section_item
        gram_block = jnp.dot(jac_block.T.astype(jnp.float32), jac_block.astype(jnp.float32), preferred_element_type=jnp.float32)
        later_section = jnp.where(section_index > 0, 1.0, 0.0).astype(jnp.float32)
        hess_block = gram_block + jnp.diag(damp_row) + later_section * identity
        hess_block = hess_block - tproduct(link_prev, link_prev)
        factor = jnp.linalg.cholesky(hess_block)
        solved = lower_solve(factor, column - tproduct(link_prev, solved_prev))
        link_next = lower_solve(factor, coupling_of(jac_block, section_index))
        return ((link_next, solved), (factor, solved))
    initial = (jnp.zeros((NS, NS), jnp.float32), jnp.zeros((NS, RHS), jnp.float32))
    _, (factors, solved_all) = lax.scan(forward, initial, (jacobians, damping, columns, section_ids))

    def backward(following, section_item):
        factor, solved, jac_block, section_index = section_item
        link_next = lower_solve(factor, coupling_of(jac_block, section_index))
        carried = jnp.dot(link_next.astype(jnp.float32), following.astype(jnp.float32), precision=HIGHEST, preferred_element_type=jnp.float32)
        value = upper_solve(factor, solved - carried)
        return (value, value)
    _, values = lax.scan(backward, jnp.zeros((NS, RHS), jnp.float32), (factors, solved_all, jacobians, section_ids), reverse=True)
    return jnp.transpose(values, (2, 0, 1))
```

```python
import functools

import jax
import jax.numpy as jnp
from jax import lax
from jax.experimental import pallas as pl
from jax.experimental.pallas import tpu as pltpu
from jax.sharding import PartitionSpec as P

HIGHEST = lax.Precision.HIGHEST
F32 = jnp.float32
N = 256
H = 128


def nn(a, b):
    return lax.dot_general(a, b, (((1,), (0,)), ((), ())), precision=HIGHEST, preferred_element_type=F32)


def nt(a, b):
    return lax.dot_general(a, b, (((1,), (1,)), ((), ())), precision=HIGHEST, preferred_element_type=F32)


def spread(x):
    return jnp.broadcast_to(x, (8, 128))


def inverse_of(x):
    guess = pl.reciprocal(x, approx=True)
    return guess + guess * (1.0 - x * guess)


def sweep8(entries):
    get = lambda i, j: entries[(min(i, j), max(i, j))]
    for a in range(0, 8, 2):
        b = a + 1
        aa, ab, bb = get(a, a), get(a, b), get(b, b)
        scale = inverse_of(aa * bb - ab * ab)
        others = [i for i in range(8) if i not in (a, b)]
        part = {i: (bb * get(i, a) - ab * get(i, b), aa * get(i, b) - ab * get(i, a)) for i in others}
        new = {}
        for place, i in enumerate(others):
            for j in others[place:]:
                new[(i, j)] = get(i, j) - (part[i][0] * get(j, a) + part[i][1] * get(j, b)) * scale
        for i in others:
            new[(min(i, a), max(i, a))] = part[i][0] * scale
            new[(min(i, b), max(i, b))] = part[i][1] * scale
        new[(a, a)], new[(b, b)], new[(a, b)] = -bb * scale, -aa * scale, ab * scale
        entries = new
    return entries


def tree_sum(terms):
    while len(terms) > 1:
        terms = [terms[i] + terms[i + 1] for i in range(0, len(terms), 2)]
    return terms[0]


def sweep(ref):
    lane = lax.broadcasted_iota(jnp.int32, (8, 128), 1)
    sub = lax.broadcasted_iota(jnp.int32, (8, 128), 0)
    rows = [ref[8 * g : 8 * g + 8, :] for g in range(16)]
    for w in range(16):
        k0 = 8 * w
        pivots = rows[w]
        cols = [spread(pivots[:, k0 + j : k0 + j + 1]) for j in range(8)]
        entries = {(i, j): spread(cols[j][i : i + 1, :]) for j in range(8) for i in range(j + 1)}
        inside = (lane >= k0) & (lane < k0 + 8)
        panel = []
        for j in range(8):
            row = spread(pivots[j : j + 1, :])
            panel.append(jnp.where(inside, jnp.where(lane == k0 + j, -1.0, 0.0), row))
        swept = sweep8(entries)
        minus = [tree_sum([swept[(min(i, j), max(i, j))] * panel[j] for j in range(8)]) for i in range(8)]
        for g in list(range(w + 1, 16)) + list(range(w)):
            terms = [spread(rows[g][:, k0 + j : k0 + j + 1]) * minus[j] for j in range(8)]
            rows[g] = jnp.where(inside, 0.0, rows[g]) + tree_sum(terms)
        new = minus[7]
        for i in range(6, -1, -1):
            new = jnp.where(sub == i, minus[i], new)
        rows[w] = -new
    for g in range(16):
        ref[8 * g : 8 * g + 8, :] = rows[g]


def kernel(
    width, peers, levels,
    jac, damp, rhs, out,
    whole, diag, links, half, gain, t_out, r_out, c_out, t_in, r_in, x_own, x_in,
    j_send, j_recv, m_send, t_recv, a_recv, x_send, x_recv,
):
    pos = lax.axis_index("tm")
    me = lax.axis_index("rhs")

    def is_multiple(step):
        return pos % step == 0

    barrier = pltpu.get_barrier_semaphore()
    count = peers - 1
    for d in range(1, peers):
        pl.semaphore_signal(barrier, inc=1, device_id={"rhs": (me + d) % peers}, device_id_type=pl.DeviceIdType.MESH)
    for level in range(levels):
        step = 2**level
        for sign in (-1, 1):
            there = pos + sign * step
            partner = is_multiple(step) & (there >= 0) & (there < width)
            count = count + partner.astype(jnp.int32)

            @pl.when(partner)
            def _(there=there):
                pl.semaphore_signal(barrier, inc=1, device_id={"tm": there}, device_id_type=pl.DeviceIdType.MESH)
    pl.semaphore_wait(barrier, count)

    depth = jac.shape[1]
    mine = pl.ds(pl.multiple_of(me * depth, depth), depth)

    def row_copy(d):
        return pltpu.make_async_remote_copy(
            src_ref=jac, dst_ref=whole.at[:, mine, :], send_sem=j_send.at[d - 1], recv_sem=j_recv.at[d - 1],
            device_id={"rhs": (me + d) % peers}, device_id_type=pl.DeviceIdType.MESH,
        )

    for d in range(1, peers):
        row_copy(d).start()
    whole[:, mine, :] = jac[...]
    for d in range(1, peers):
        row_copy(d).wait()

    on_diag = lax.broadcasted_iota(jnp.int32, (N, N), 0) == lax.broadcasted_iota(jnp.int32, (N, N), 1)
    first = jnp.where(pos > 0, 1.0, 0.0).astype(F32)
    for k in range(2):
        block = lax.dot_general(whole[k], whole[k], (((0,), (0,)), ((), ())), preferred_element_type=F32)
        extra = damp[k : k + 1, :] + (first if k == 0 else 1.0)
        block = block + jnp.where(on_diag, jnp.broadcast_to(extra, (N, N)), 0.0)
        diag[k, 0] = block[:H, :H]
        diag[k, 1] = block[H:, :H]
        diag[k, 2] = block[H:, H:]
    last = jnp.where(pos < width - 1, 1.0, 0.0).astype(F32)
    links[1, 0:N, :] = -whole[0].astype(F32).T
    links[1, N : 2 * N, :] = -whole[1].astype(F32) * last
    for k in range(2):
        links[k, 2 * N : 2 * N + 8, :] = rhs[:, k, :]

    def message(t, blk, side, place, hop, part):
        slot = 1 - side
        if part < 3:
            src, dst, sem = t_out.at[blk, side, part], t_in.at[t, slot, part], t_recv.at[t, slot, part]
        elif part == 3:
            src, dst, sem = r_out.at[blk, side], r_in.at[t, slot], t_recv.at[t, slot, 3]
        else:
            dst = links.at[0, pl.ds(pl.multiple_of(slot * N, N), N), :]
            src, sem = c_out.at[blk], a_recv.at[slot]
        return pltpu.make_async_remote_copy(
            src_ref=src, dst_ref=dst, send_sem=m_send.at[blk, place, part], recv_sem=sem,
            device_id={"tm": pos + hop * (2 * side - 1)}, device_id_type=pl.DeviceIdType.MESH,
        )

    def exists(there):
        return (there >= 0) & (there < width)

    def next_odd_side(t, step):
        quarter = jnp.where(t == 0, 2 * pos + 1, pos // step) % 4
        return jnp.where(quarter == 1, 1, 0)

    def absorb(t, part):
        def take(slot):
            arrival = message(t - 1, 0, 1 - slot, 0, 1, part)
            arrival.wait_recv()
            if part < 3:
                diag[0, part] = diag[0, part] - t_in[t - 1, slot, part]
            else:
                links[0, 2 * N : 2 * N + 8, :] = links[0, 2 * N : 2 * N + 8, :] - r_in[t - 1, slot]

        @pl.when(pos > 0)
        def _():
            take(0)

        @pl.when(t >= 2)
        def _():
            take(1)

    def products(t, blk, step):
        side_o = next_odd_side(t, step)
        hop = jnp.where(t == 0, 1, step)
        for place in range(2):
            side = side_o if place == 0 else 1 - side_o
            rows_at = pl.multiple_of(side * N, N)
            there = pos + hop * (2 * side - 1)
            local = (t == 0) & (side == 0)
            remote = exists(there) & jnp.logical_not(local)

            for part, (r, c) in enumerate(((0, 0), (1, 0), (1, 1))):
                left = gain[blk, pl.ds(rows_at + r * H, H), :]
                right = links[blk, pl.ds(rows_at + c * H, H), :]
                t_out[blk, side, part] = nt(left, right)

                @pl.when(remote)
                def _(part=part, side=side, place=place):
                    message(t, blk, side, place, hop, part).start()
            mat = links[blk, pl.ds(rows_at, N), :]
            r_out[blk, side] = nt(gain[blk, 2 * N : 2 * N + 8, :], mat)

            @pl.when(remote)
            def _(side=side, place=place):
                message(t, blk, side, place, hop, 3).start()

            if place == 0:
                other_at = pl.multiple_of((1 - side) * N, N)
                c_out[blk] = -nt(gain[blk, pl.ds(other_at, N), :], mat)

                @pl.when(remote)
                def _(side=side):
                    message(t, blk, side, 0, hop, 4).start()

            @pl.when(local)
            def _(place=place, side=side):
                for part in range(3):
                    diag[0, part] = diag[0, part] - t_out[blk, side, part]
                links[0, 2 * N : 2 * N + 8, :] = links[0, 2 * N : 2 * N + 8, :] - r_out[blk, side]
                if place == 0:
                    links[0, N : 2 * N, :] = c_out[blk]

    def wait_sent(t, blk, step):
        side_o = next_odd_side(t, step)
        hop = jnp.where(t == 0, 1, step)
        for place in range(2):
            side = side_o if place == 0 else 1 - side_o
            there = pos + hop * (2 * side - 1)
            remote = exists(there) & jnp.logical_not((t == 0) & (side == 0))

            @pl.when(remote)
            def _(side=side, place=place):
                for part in range(5 - place):
                    message(t, blk, side, place, hop, part).wait_send()

    def eliminate(t, step):
        blk = jnp.where(t == 0, 1, 0)
        active = (t >= 1) & (pos % step == 0)
        odd = (t <= levels) & active & (pos // step % 2 == 1)
        root = (t == levels + 1) & (pos == 0)
        invert = (t == 0) | odd | root

        def part_of(h, carry):
            @pl.when(active & (h == 0))
            def _():
                absorb(t, 0)

            @pl.when(active & (h == 1))
            def _():
                for part in (1, 2, 3):
                    absorb(t, part)

            @pl.when(invert & (h == 1))
            def _():
                half[...] = -nn(diag[blk, 1], diag[blk, 0])
                diag[blk, 2] = diag[blk, 2] - nt(half[...], diag[blk, 1])

            @pl.when(invert)
            def _():
                sweep(diag.at[blk, 2 * h])

            return carry

        lax.fori_loop(0, 2, part_of, 0)

        def gains(start, size):
            low = links[blk, start : start + size, :H]
            rest = links[blk, start : start + size, H:] - nt(low, half[...])
            upper = -nn(rest, diag[blk, 2])
            gain[blk, start : start + size, H:] = upper
            gain[blk, start : start + size, :H] = -nn(low, diag[blk, 0]) - nn(upper, half[...])

        @pl.when(odd)
        def _():
            message(t - 1, 0, 1, 0, 1, 4).wait_recv()

            @pl.when(t >= 2)
            def _():
                message(t - 1, 0, 0, 0, 1, 4).wait_recv()

        @pl.when(odd | (t == 0))
        def _():
            gains(0, 2 * N + 8)
            products(t, blk, step)

        @pl.when(odd)
        def _():
            wait_sent(t, blk, step)

        @pl.when(root)
        def _():
            gains(2 * N, 8)

        return jnp.where(t == 0, 1, 2 * step)

    lax.fori_loop(0, levels + 2, eliminate, jnp.int32(1))

    def x_copy(there, slot, index):
        return pltpu.make_async_remote_copy(
            src_ref=x_own, dst_ref=x_in.at[slot], send_sem=x_send.at[index], recv_sem=x_recv.at[slot],
            device_id={"tm": there}, device_id_type=pl.DeviceIdType.MESH,
        )

    def x_targets(level):
        targets = []
        for lower in reversed(range(level)):
            step = 2**lower
            targets.append((pos + step, 0, 2 * lower))
            if lower > 0:
                targets.append((pos - step, 1, 2 * lower + 1))
        targets.append((pos - 1, 2, 1))
        return targets

    def start_x(level):
        for there, slot, index in x_targets(level):
            @pl.when(exists(there))
            def _(there=there, slot=slot, index=index):
                x_copy(there, slot, index).start()

    def wait_x(level):
        for there, slot, index in x_targets(level):
            @pl.when(exists(there))
            def _(there=there, slot=slot, index=index):
                x_copy(there, slot, index).wait_send()

    @pl.when(pos == 0)
    def _():
        x_own[...] = gain[0, 2 * N : 2 * N + 8, :]
        start_x(levels)

    for level in reversed(range(levels)):
        step = 2**level

        @pl.when(pos % (2 * step) == step)
        def _(level=level, step=step):
            side_o = next_odd_side(1, step)
            x_own[...] = gain[0, 2 * N : 2 * N + 8, :]
            for side in (1 - side_o, side_o):
                @pl.when((side == 0) | (pos + step < width))
                def _(side=side):
                    slot = side * (2 if level == 0 else 1)
                    x_copy(pos, slot, 0).wait_recv()
                    x_own[...] = x_own[...] - nn(x_in[slot], gain[0, pl.ds(pl.multiple_of(side * N, N), N), :])
            start_x(level)

    out[:, 0, :] = x_own[...]
    out[:, 1, :] = gain[1, 2 * N : 2 * N + 8, :] - nn(x_own[...], gain[1, 0:N, :])

    @pl.when(pos < width - 1)
    def _():
        @pl.when(pos % 2 == 0)
        def _():
            x_copy(pos, 2, 0).wait_recv()

        out[:, 1, :] = out[:, 1, :] - nn(x_in[2], gain[1, N : 2 * N, :])

    wait_sent(jnp.int32(0), 1, jnp.int32(1))

    @pl.when(pos == 0)
    def _():
        wait_x(levels)

    for level in range(levels):
        @pl.when(pos % (2 * 2**level) == 2**level)
        def _(level=level):
            wait_x(level)


def per_device(jacobians, damping, right_sides):
    width = lax.axis_size("tm")
    peers = lax.axis_size("rhs")
    levels = width.bit_length() - 1
    vmem = pl.BlockSpec(memory_space=pltpu.VMEM)
    return pl.pallas_call(
        functools.partial(kernel, width, peers, levels),
        out_shape=jax.ShapeDtypeStruct(right_sides.shape, F32),
        in_specs=[vmem] * 3,
        out_specs=vmem,
        scratch_shapes=[
            pltpu.VMEM((2, N, N), jnp.bfloat16),
            pltpu.VMEM((2, 3, H, H), F32),
            pltpu.VMEM((2, 2 * N + 8, N), F32),
            pltpu.VMEM((H, H), F32),
            pltpu.VMEM((2, 2 * N + 8, N), F32),
            pltpu.VMEM((2, 2, 3, H, H), F32),
            pltpu.VMEM((2, 2, 8, N), F32),
            pltpu.VMEM((2, N, N), F32),
            pltpu.VMEM((levels + 1, 2, 3, H, H), F32),
            pltpu.VMEM((levels + 1, 2, 8, N), F32),
            pltpu.VMEM((8, N), F32),
            pltpu.VMEM((3, 8, N), F32),
            pltpu.SemaphoreType.DMA((peers - 1,)),
            pltpu.SemaphoreType.DMA((peers - 1,)),
            pltpu.SemaphoreType.DMA((2, 2, 5)),
            pltpu.SemaphoreType.DMA((levels + 1, 2, 4)),
            pltpu.SemaphoreType.DMA((2,)),
            pltpu.SemaphoreType.DMA((2 * levels,)),
            pltpu.SemaphoreType.DMA((3,)),
        ],
        compiler_params=pltpu.CompilerParams(
            collective_id=0, has_side_effects=True, vmem_limit_bytes=32 * 1024 * 1024
        ),
    )(jacobians, damping, right_sides)


def solution(mesh):
    in_specs = (P("tm", "rhs", None), P("tm", None), P("rhs", "tm", None))
    return jax.shard_map(
        per_device, mesh=mesh, in_specs=in_specs, out_specs=P("rhs", "tm", None), check_vma=False
    )
```

```python
import functools

import jax
import jax.numpy as jnp
from jax import lax
from jax.experimental import pallas as pl
from jax.experimental.pallas import tpu as pltpu
from jax.sharding import PartitionSpec as P

HIGHEST = lax.Precision.HIGHEST
F32 = jnp.float32
N = 256
H = 128


def nn(a, b):
    return lax.dot_general(a, b, (((1,), (0,)), ((), ())), precision=HIGHEST, preferred_element_type=F32)


def nt(a, b):
    return lax.dot_general(a, b, (((1,), (1,)), ((), ())), precision=HIGHEST, preferred_element_type=F32)


def spread(x):
    return jnp.broadcast_to(x, (8, 128))


def tree_sum(terms):
    while len(terms) > 1:
        terms = [terms[i] + terms[i + 1] for i in range(0, len(terms), 2)]
    return terms[0]


def sweep8(cols, sub):
    for a in range(0, 8, 2):
        b = a + 1
        row_a = [spread(c[a : a + 1, :]) for c in cols]
        row_b = [spread(c[b : b + 1, :]) for c in cols]
        aa, ab, bb = row_a[a], row_a[b], row_b[b]
        det = aa * bb - ab * ab
        guess = pl.reciprocal(det, approx=True)
        mend = 2.0 - det * guess
        is_a, is_b = sub == a, sub == b
        part_a = jnp.where(is_a, -bb, jnp.where(is_b, ab, bb * cols[a] - ab * cols[b])) * guess
        part_b = jnp.where(is_a, ab, jnp.where(is_b, -aa, aa * cols[b] - ab * cols[a])) * guess
        new = []
        for j in range(8):
            if j == a:
                new.append(part_a * mend)
            elif j == b:
                new.append(part_b * mend)
            else:
                kept = jnp.where(is_a | is_b, 0.0, cols[j])
                new.append(kept - (part_a * row_a[j] + part_b * row_b[j]) * mend)
        cols = new
    return cols


def sweep(ref):
    lane = lax.broadcasted_iota(jnp.int32, (8, 128), 1)
    sub = lax.broadcasted_iota(jnp.int32, (8, 128), 0)
    rows = [ref[8 * g : 8 * g + 8, :] for g in range(16)]
    for start in (0, 8):
        panel = range(start, start + 8)
        for w in panel:
            k0 = 8 * w
            inside = (lane >= k0) & (lane < k0 + 8)
            pivots = rows[w]
            cols = sweep8([spread(pivots[:, k0 + j : k0 + j + 1]) + 0.0 for j in range(8)], sub)
            terms = []
            for j in range(8):
                row = jnp.where(inside, jnp.where(lane == k0 + j, -1.0, 0.0), spread(pivots[j : j + 1, :]))
                terms.append(cols[j] * row)
            swept = tree_sum(terms)
            minus = [spread(swept[j : j + 1, :]) for j in range(8)]
            for g in list(range(w + 1, start + 8)) + list(range(start, w)):
                terms = [spread(rows[g][:, k0 + j : k0 + j + 1]) * minus[j] for j in range(8)]
                rows[g] = jnp.where(inside, 0.0, rows[g]) + tree_sum(terms)
            rows[w] = -swept
        others = range(8 - start, 16 - start)
        zero = jnp.zeros((8, 128), F32)
        far = jnp.concatenate([rows[g] for g in others], axis=0)
        near = jnp.concatenate([rows[g] if g in panel else zero for g in range(16)], axis=0)
        change = nn(far, near)
        inside = (lane >= 8 * start) & (lane < 8 * start + 64)
        for index, g in enumerate(others):
            rows[g] = jnp.where(inside, 0.0, rows[g]) - change[8 * index : 8 * index + 8, :]
    for g in range(16):
        ref[8 * g : 8 * g + 8, :] = rows[g]


def kernel(
    width, peers, levels,
    jac, damp, rhs, out,
    whole, damp_in, rhs_in, diag, links, half, full, gain, t_out, r_out, c_out, t_in, r_in,
    d_in, d_rhs, x_root, x_own, x_in,
    i_sem, j_send, j_recv, m_send, t_recv, a_recv, p_send, p_recv, d_send, d_recv, z_send, x_send, x_recv,
):
    pos = lax.axis_index("tm")
    me = lax.axis_index("rhs")
    middle = width // 2
    core = me % 2

    def is_multiple(step):
        return pos % step == 0

    depth = jac.shape[1]
    mine = pl.ds(pl.multiple_of(me * depth, depth), depth)
    loads = [
        pltpu.make_async_copy(jac, whole.at[:, mine, :], i_sem.at[0]),
        pltpu.make_async_copy(damp, damp_in, i_sem.at[1]),
        pltpu.make_async_copy(rhs, rhs_in, i_sem.at[2]),
    ]
    for load in loads:
        load.start()

    barrier = pltpu.get_barrier_semaphore()
    count = peers - 1
    for d in range(1, peers):
        pl.semaphore_signal(barrier, inc=1, device_id={"rhs": (me + d) % peers}, device_id_type=pl.DeviceIdType.MESH)
    partners = [((pos + sign * 2**k), is_multiple(2**k)) for k in range(levels) for sign in (-1, 1)]
    for k in range(levels - 2):
        partners.append((jnp.int32(2**k), pos == middle))
        partners.append((jnp.int32(middle), pos == 2**k))
    for there, holds in partners:
        partner = holds & (there >= 0) & (there < width)
        count = count + partner.astype(jnp.int32)

        @pl.when(partner)
        def _(there=there):
            pl.semaphore_signal(barrier, inc=1, device_id={"tm": there}, device_id_type=pl.DeviceIdType.MESH)
    pl.semaphore_wait(barrier, count)

    def row_copy(d):
        return pltpu.make_async_remote_copy(
            src_ref=jac, dst_ref=whole.at[:, mine, :], send_sem=j_send.at[d - 1], recv_sem=j_recv.at[d - 1],
            device_id={"rhs": (me + d) % peers}, device_id_type=pl.DeviceIdType.MESH,
        )

    for d in range(1, peers):
        row_copy(d).start()
    for load in loads:
        load.wait()
    for d in range(1, peers):
        row_copy(d).wait()

    on_diag = lax.broadcasted_iota(jnp.int32, (N, N), 0) == lax.broadcasted_iota(jnp.int32, (N, N), 1)
    first = jnp.where(pos > 0, 1.0, 0.0).astype(F32)
    for k in range(2):
        block = lax.dot_general(whole[k], whole[k], (((0,), (0,)), ((), ())), preferred_element_type=F32)
        extra = damp_in[k : k + 1, :] + (first if k == 0 else 1.0)
        block = block + jnp.where(on_diag, jnp.broadcast_to(extra, (N, N)), 0.0)
        diag[k, 0] = block[:H, :H]
        diag[k, 1] = block[H:, :H]
        diag[k, 2] = block[H:, H:]
    last = jnp.where(pos < width - 1, 1.0, 0.0).astype(F32)
    links[1, 0:N, :] = -whole[0].astype(F32).T
    links[1, N : 2 * N, :] = -whole[1].astype(F32) * last
    for k in range(2):
        links[k, 2 * N : 2 * N + 8, :] = rhs_in[:, k, :]

    def coupling_half(slot, which):
        return links.at[0, pl.ds(pl.multiple_of(slot * N + which * H, H), H), :]

    def pair_copy(slot):
        return pltpu.make_async_remote_copy(
            src_ref=coupling_half(slot, core), dst_ref=coupling_half(slot, core), send_sem=p_send.at[slot],
            recv_sem=p_recv.at[slot], device_id={"rhs": me + 1 - 2 * core}, device_id_type=pl.DeviceIdType.MESH,
        )

    def root_copy(part):
        if part < 3:
            src, dst = diag.at[0, part], d_in.at[part]
        else:
            src, dst = links.at[0, 2 * N : 2 * N + 8, :], d_rhs
        return pltpu.make_async_remote_copy(
            src_ref=src, dst_ref=dst, send_sem=d_send.at[part], recv_sem=d_recv.at[part],
            device_id={"tm": middle}, device_id_type=pl.DeviceIdType.MESH,
        )

    def message(t, blk, side, place, hop, part):
        slot = 1 - side
        if part < 3:
            src, dst, sem = t_out.at[blk, side, part], t_in.at[t, slot, part], t_recv.at[t, slot, part]
        elif part == 3:
            src, dst, sem = r_out.at[blk, side], r_in.at[t, slot], t_recv.at[t, slot, 3]
        else:
            dst = coupling_half(slot, core)
            src, sem = c_out.at[blk], a_recv.at[slot]
        return pltpu.make_async_remote_copy(
            src_ref=src, dst_ref=dst, send_sem=m_send.at[blk, place, part], recv_sem=sem,
            device_id={"tm": pos + hop * (2 * side - 1)}, device_id_type=pl.DeviceIdType.MESH,
        )

    def exists(there):
        return (there >= 0) & (there < width)

    def next_odd_side(t, step):
        quarter = jnp.where(t == 0, 2 * pos + 1, pos // step) % 4
        return jnp.where(quarter == 1, 1, 0)

    def absorb(t, part):
        def take(slot):
            arrival = message(t - 1, 0, 1 - slot, 0, 1, part)
            arrival.wait_recv()
            if part < 3:
                diag[0, part] = diag[0, part] - t_in[t - 1, slot, part]
            else:
                links[0, 2 * N : 2 * N + 8, :] = links[0, 2 * N : 2 * N + 8, :] - r_in[t - 1, slot]

        @pl.when(pos > 0)
        def _():
            take(0)

        @pl.when(t >= 2)
        def _():
            take(1)

    def products(t, blk, step):
        side_o = next_odd_side(t, step)
        hop = jnp.where(t == 0, 1, step)
        last = t == levels
        y_rows = slice(2 * N, 2 * N + 8)

        def gains(start, size):
            rows = pl.ds(start, size)
            gain[blk, rows, :] = nn(links[blk, rows, :], full[...])

        for place in range(2):
            side = side_o if place == 0 else 1 - side_o
            at = pl.multiple_of(side * N, N)
            other_at = pl.multiple_of((1 - side) * N, N)
            there = pos + hop * (2 * side - 1)
            local = (t == 0) & (side == 0)
            remote = exists(there) & jnp.logical_not(local | last)

            def send(part):
                @pl.when(remote)
                def _():
                    message(t, blk, side, place, hop, part).start()

            def give():
                for part, (r, c) in enumerate(((0, 0), (1, 0), (1, 1))):
                    left = pl.ds(pl.multiple_of(at + r * H, H), H)
                    right = pl.ds(pl.multiple_of(at + c * H, H), H)
                    if part < 2:
                        gains(pl.multiple_of(at + r * H, H), H)
                    t_out[blk, side, part] = nt(gain[blk, left, :], links[blk, right, :])
                    send(part)
                if place == 0:
                    gains(2 * N, 8)
                mat = links[blk, pl.ds(at, N), :]
                r_out[blk, side] = nt(gain[blk, y_rows, :], mat)
                send(3)

                if place == 0:
                    own = pl.ds(pl.multiple_of(other_at + core * H, H), H)
                    gains(pl.multiple_of(other_at + core * H, H), H)
                    c_out[blk] = -nt(gain[blk, own, :], mat)
                    send(4)

                @pl.when(local)
                def _():
                    for part in range(3):
                        diag[0, part] = diag[0, part] - t_out[blk, side, part]
                    links[0, y_rows, :] = links[0, y_rows, :] - r_out[blk, side]
                    if place == 0:
                        gains(other_at, N)
                        links[0, N : 2 * N, :] = -nt(gain[blk, pl.ds(other_at, N), :], mat)

            if place == 0:
                pl.when(jnp.logical_not(last))(give)

                @pl.when(last)
                def _():
                    gains(2 * N, 8)
            else:
                give()

        @pl.when(last)
        def _():
            for part in range(4):
                root_copy(part).wait_recv()
            for part in range(3):
                diag[0, part] = d_in[part] - t_out[blk, 0, part]
            d_rhs[...] = d_rhs[...] - r_out[blk, 0]

    def wait_sent(t, blk, step):
        side_o = next_odd_side(t, step)
        hop = jnp.where(t == 0, 1, step)
        for place in range(2):
            side = side_o if place == 0 else 1 - side_o
            there = pos + hop * (2 * side - 1)
            remote = exists(there) & jnp.logical_not(((t == 0) & (side == 0)) | (t == levels))

            @pl.when(remote)
            def _(side=side, place=place):
                for part in range(5 - place):
                    message(t, blk, side, place, hop, part).wait_send()

    def eliminate(t, step):
        blk = jnp.where(t == 0, 1, 0)
        active = (t >= 1) & (t <= levels) & (pos % step == 0)
        odd = active & (pos // step % 2 == 1)
        root = (t == levels + 1) & (pos == middle)
        invert = (t == 0) | odd | root

        def part_of(h, carry):
            @pl.when(active & (h == 0))
            def _():
                absorb(t, 0)

            @pl.when(active & (h == 1))
            def _():
                for part in (1, 2, 3):
                    absorb(t, part)

            @pl.when(invert & (h == 1))
            def _():
                half[...] = -nn(diag[blk, 1], diag[blk, 0])
                diag[blk, 2] = diag[blk, 2] - nt(half[...], diag[blk, 1])

            @pl.when(invert)
            def _():
                sweep(diag.at[blk, 2 * h])

            return carry

        lax.fori_loop(0, 2, part_of, 0)

        @pl.when((t == levels) & (pos == 0))
        def _():
            for part in range(4):
                root_copy(part).start()

        def each_coupling(act):
            @pl.when(odd)
            def _():
                act(0)

                @pl.when(t >= 2)
                def _():
                    act(1)

        def hand_on(slot):
            message(t - 1, 0, 1 - slot, 0, 1, 4).wait_recv()
            pair_copy(slot).start()

        each_coupling(hand_on)

        @pl.when(invert)
        def _():
            lower = nn(diag[blk, 2], half[...])
            upper = lower.T
            full[H:, H:] = -diag[blk, 2]
            full[H:, :H] = lower
            full[:H, H:] = upper
            full[:H, :H] = -diag[blk, 0] - nn(upper, half[...])

        each_coupling(lambda slot: pair_copy(slot).wait_recv())

        @pl.when(odd | (t == 0))
        def _():
            products(t, blk, step)

        @pl.when(odd)
        def _():
            wait_sent(t, blk, step)

        each_coupling(lambda slot: pair_copy(slot).wait_send())

        @pl.when(root)
        def _():
            x_root[...] = nn(d_rhs[...], full[...])

        return jnp.where(t == 0, 1, 2 * step)

    lax.fori_loop(0, levels + 2, eliminate, jnp.int32(1))

    def x_copy(there, slot, index):
        return pltpu.make_async_remote_copy(
            src_ref=x_own, dst_ref=x_in.at[slot], send_sem=x_send.at[index], recv_sem=x_recv.at[slot],
            device_id={"tm": there}, device_id_type=pl.DeviceIdType.MESH,
        )

    def x_targets(level):
        targets = []
        for lower in reversed(range(level)):
            step = 2**lower
            targets.append((pos + step, 0, 2 * lower))
            if lower > 0:
                targets.append((pos - step, 1, 2 * lower + 1))
        targets.append((pos - 1, 2, 1))
        return targets

    def start_x(level):
        for there, slot, index in x_targets(level):
            @pl.when(exists(there))
            def _(there=there, slot=slot, index=index):
                x_copy(there, slot, index).start()

    def wait_x(level):
        for there, slot, index in x_targets(level):
            @pl.when(exists(there))
            def _(there=there, slot=slot, index=index):
                x_copy(there, slot, index).wait_send()

    def first_copy(k):
        there = 2**k if k < levels - 1 else 0
        return pltpu.make_async_remote_copy(
            src_ref=x_root, dst_ref=x_in.at[0], send_sem=z_send.at[k], recv_sem=x_recv.at[0],
            device_id={"tm": there}, device_id_type=pl.DeviceIdType.MESH,
        )

    @pl.when(pos == middle)
    def _():
        for k in reversed(range(levels - 1)):
            first_copy(k).start()
        first_copy(levels - 1).start()
        x_own[...] = gain[0, 2 * N : 2 * N + 8, :] - nn(x_root[...], gain[0, 0:N, :])
        start_x(levels - 1)

    @pl.when(pos == 0)
    def _():
        x_copy(pos, 0, 0).wait_recv()
        x_own[...] = x_in[0]

    for level in reversed(range(levels - 1)):
        step = 2**level

        @pl.when(pos % (2 * step) == step)
        def _(level=level, step=step):
            side_o = next_odd_side(1, step)
            x_own[...] = gain[0, 2 * N : 2 * N + 8, :]
            for side in (1 - side_o, side_o):
                @pl.when((side == 0) | (pos + step < width))
                def _(side=side):
                    slot = side * (2 if level == 0 else 1)
                    x_copy(pos, slot, 0).wait_recv()
                    x_own[...] = x_own[...] - nn(x_in[slot], gain[0, pl.ds(pl.multiple_of(side * N, N), N), :])
            start_x(level)

    out[:, 0, :] = x_own[...]
    out[:, 1, :] = gain[1, 2 * N : 2 * N + 8, :] - nn(x_own[...], gain[1, 0:N, :])

    @pl.when(pos < width - 1)
    def _():
        @pl.when(pos % 2 == 0)
        def _():
            x_copy(pos, 2, 0).wait_recv()

        out[:, 1, :] = out[:, 1, :] - nn(x_in[2], gain[1, N : 2 * N, :])

    wait_sent(jnp.int32(0), 1, jnp.int32(1))

    @pl.when(pos == 0)
    def _():
        for part in range(4):
            root_copy(part).wait_send()

    @pl.when(pos == middle)
    def _():
        for k in range(levels):
            first_copy(k).wait_send()
        wait_x(levels - 1)

    for level in range(levels - 1):
        @pl.when(pos % (2 * 2**level) == 2**level)
        def _(level=level):
            wait_x(level)


def per_device(jacobians, damping, right_sides):
    width = lax.axis_size("tm")
    peers = lax.axis_size("rhs")
    levels = width.bit_length() - 1
    vmem = pl.BlockSpec(memory_space=pltpu.VMEM)
    return pl.pallas_call(
        functools.partial(kernel, width, peers, levels),
        out_shape=jax.ShapeDtypeStruct(right_sides.shape, F32),
        in_specs=[pl.BlockSpec(memory_space=pl.ANY)] * 3,
        out_specs=vmem,
        scratch_shapes=[
            pltpu.VMEM((2, N, N), jnp.bfloat16),
            pltpu.VMEM(damping.shape, F32),
            pltpu.VMEM(right_sides.shape, F32),
            pltpu.VMEM((2, 3, H, H), F32),
            pltpu.VMEM((2, 2 * N + 8, N), F32),
            pltpu.VMEM((H, H), F32),
            pltpu.VMEM((N, N), F32),
            pltpu.VMEM((2, 2 * N + 8, N), F32),
            pltpu.VMEM((2, 2, 3, H, H), F32),
            pltpu.VMEM((2, 2, 8, N), F32),
            pltpu.VMEM((2, H, N), F32),
            pltpu.VMEM((levels, 2, 3, H, H), F32),
            pltpu.VMEM((levels, 2, 8, N), F32),
            pltpu.VMEM((3, H, H), F32),
            pltpu.VMEM((8, N), F32),
            pltpu.VMEM((8, N), F32),
            pltpu.VMEM((8, N), F32),
            pltpu.VMEM((3, 8, N), F32),
            pltpu.SemaphoreType.DMA((3,)),
            pltpu.SemaphoreType.DMA((peers - 1,)),
            pltpu.SemaphoreType.DMA((peers - 1,)),
            pltpu.SemaphoreType.DMA((2, 2, 5)),
            pltpu.SemaphoreType.DMA((levels, 2, 4)),
            pltpu.SemaphoreType.DMA((2,)),
            pltpu.SemaphoreType.DMA((2,)),
            pltpu.SemaphoreType.DMA((2,)),
            pltpu.SemaphoreType.DMA((4,)),
            pltpu.SemaphoreType.DMA((4,)),
            pltpu.SemaphoreType.DMA((levels,)),
            pltpu.SemaphoreType.DMA((2 * levels,)),
            pltpu.SemaphoreType.DMA((3,)),
        ],
        compiler_params=pltpu.CompilerParams(
            collective_id=0, has_side_effects=True, vmem_limit_bytes=32 * 1024 * 1024
        ),
    )(jacobians, damping, right_sides)


def solution(mesh):
    in_specs = (P("tm", "rhs", None), P("tm", None), P("rhs", "tm", None))
    return jax.shard_map(
        per_device, mesh=mesh, in_specs=in_specs, out_specs=P("rhs", "tm", None), check_vma=False
    )
```

```python
import functools

import jax
import jax.numpy as jnp
from jax import lax
from jax.experimental import pallas as pl
from jax.experimental.pallas import tpu as pltpu
from jax.sharding import PartitionSpec as P

HIGHEST = lax.Precision.HIGHEST
F32 = jnp.float32
N = 256
H = 128


def nn(a, b):
    return lax.dot_general(a, b, (((1,), (0,)), ((), ())), precision=HIGHEST, preferred_element_type=F32)


def nt(a, b):
    return lax.dot_general(a, b, (((1,), (1,)), ((), ())), precision=HIGHEST, preferred_element_type=F32)


def spread(x):
    return jnp.broadcast_to(x, (8, 128))


def tree_sum(terms):
    while len(terms) > 1:
        terms = [terms[i] + terms[i + 1] for i in range(0, len(terms), 2)]
    return terms[0]


def sweep8(cols, sub):
    for a in range(0, 8, 2):
        b = a + 1
        row_a = [spread(c[a : a + 1, :]) for c in cols]
        row_b = [spread(c[b : b + 1, :]) for c in cols]
        aa, ab, bb = row_a[a], row_a[b], row_b[b]
        det = aa * bb - ab * ab
        guess = pl.reciprocal(det, approx=True)
        mend = 2.0 - det * guess
        is_a, is_b = sub == a, sub == b
        part_a = jnp.where(is_a, -bb, jnp.where(is_b, ab, bb * cols[a] - ab * cols[b])) * guess
        part_b = jnp.where(is_a, ab, jnp.where(is_b, -aa, aa * cols[b] - ab * cols[a])) * guess
        new = []
        for j in range(8):
            if j == a:
                new.append(part_a * mend)
            elif j == b:
                new.append(part_b * mend)
            else:
                kept = jnp.where(is_a | is_b, 0.0, cols[j])
                new.append(kept - (part_a * row_a[j] + part_b * row_b[j]) * mend)
        cols = new
    return cols


def sweep(ref):
    lane = lax.broadcasted_iota(jnp.int32, (8, 128), 1)
    sub = lax.broadcasted_iota(jnp.int32, (8, 128), 0)
    rows = [ref[8 * g : 8 * g + 8, :] for g in range(16)]
    for start in (0, 8):
        panel = range(start, start + 8)
        for w in panel:
            k0 = 8 * w
            inside = (lane >= k0) & (lane < k0 + 8)
            pivots = rows[w]
            cols = sweep8([spread(pivots[:, k0 + j : k0 + j + 1]) + 0.0 for j in range(8)], sub)
            terms = []
            for j in range(8):
                row = jnp.where(inside, jnp.where(lane == k0 + j, -1.0, 0.0), spread(pivots[j : j + 1, :]))
                terms.append(cols[j] * row)
            swept = tree_sum(terms)
            minus = [spread(swept[j : j + 1, :]) for j in range(8)]
            for g in list(range(w + 1, start + 8)) + list(range(start, w)):
                terms = [spread(rows[g][:, k0 + j : k0 + j + 1]) * minus[j] for j in range(8)]
                rows[g] = jnp.where(inside, 0.0, rows[g]) + tree_sum(terms)
            rows[w] = -swept
        others = range(8 - start, 16 - start)
        zero = jnp.zeros((8, 128), F32)
        far = jnp.concatenate([rows[g] for g in others], axis=0)
        near = jnp.concatenate([rows[g] if g in panel else zero for g in range(16)], axis=0)
        change = nn(far, near)
        inside = (lane >= 8 * start) & (lane < 8 * start + 64)
        for index, g in enumerate(others):
            rows[g] = jnp.where(inside, 0.0, rows[g]) - change[8 * index : 8 * index + 8, :]
    for g in range(16):
        ref[8 * g : 8 * g + 8, :] = rows[g]


def kernel(
    width, peers, levels,
    jac, damp, rhs, out,
    whole, damp_in, rhs_in, diag, links, half, full, gain, t_out, r_out, c_out, t_in, r_in,
    d_in, d_rhs, map_o, map_n, x_root, x_own, x_o, x_in,
    i_sem, j_send, j_recv, m_send, t_recv, a_recv, p_send, p_recv, d_send, d_recv, g_send, g_recv, z_send, x_send, x_recv,
):
    pos = lax.axis_index("tm")
    me = lax.axis_index("rhs")
    middle = width // 2
    tops = list(range(levels - 2, -1, -2))
    core = me % 2

    depth = jac.shape[1]
    mine = pl.ds(pl.multiple_of(me * depth, depth), depth)
    loads = [
        pltpu.make_async_copy(jac, whole.at[:, mine, :], i_sem.at[0]),
        pltpu.make_async_copy(damp, damp_in, i_sem.at[1]),
        pltpu.make_async_copy(rhs, rhs_in, i_sem.at[2]),
    ]
    for load in loads:
        load.start()

    barrier = pltpu.get_barrier_semaphore()
    count = peers - 1
    for d in range(1, peers):
        pl.semaphore_signal(barrier, inc=1, device_id={"rhs": (me + d) % peers}, device_id_type=pl.DeviceIdType.MESH)
    for sign in (-1, 1):
        there = pos + sign
        partner = (there >= 0) & (there < width)
        count = count + partner.astype(jnp.int32)

        @pl.when(partner)
        def _(there=there):
            pl.semaphore_signal(barrier, inc=1, device_id={"tm": there}, device_id_type=pl.DeviceIdType.MESH)
    pl.semaphore_wait(barrier, count)

    def row_copy(k, d):
        return pltpu.make_async_remote_copy(
            src_ref=jac.at[k], dst_ref=whole.at[k, mine, :], send_sem=j_send.at[k, d - 1], recv_sem=j_recv.at[k, d - 1],
            device_id={"rhs": (me + d) % peers}, device_id_type=pl.DeviceIdType.MESH,
        )

    for k in (1, 0):
        for d in range(1, peers):
            row_copy(k, d).start()
    for load in loads:
        load.wait()

    def local_block(k):
        for d in range(1, peers):
            row_copy(k, d).wait()
        on_diag = lax.broadcasted_iota(jnp.int32, (N, N), 0) == lax.broadcasted_iota(jnp.int32, (N, N), 1)
        block = lax.dot_general(whole[k], whole[k], (((0,), (0,)), ((), ())), preferred_element_type=F32)
        extra = damp_in[k : k + 1, :] + (jnp.where(pos > 0, 1.0, 0.0).astype(F32) if k == 0 else 1.0)
        block = block + jnp.where(on_diag, jnp.broadcast_to(extra, (N, N)), 0.0)
        diag[k, 0] = block[:H, :H]
        diag[k, 1] = block[H:, :H]
        diag[k, 2] = block[H:, H:]
        links[k, 2 * N : 2 * N + 8, :] = rhs_in[:, k, :]
        if k == 0:
            links[1, 0:N, :] = -whole[0].astype(F32).T
        else:
            last = jnp.where(pos < width - 1, 1.0, 0.0).astype(F32)
            links[1, N : 2 * N, :] = -whole[1].astype(F32) * last

    local_block(1)

    def coupling_half(slot, which):
        return links.at[0, pl.ds(pl.multiple_of(slot * N + which * H, H), H), :]

    def pair_copy(slot):
        return pltpu.make_async_remote_copy(
            src_ref=coupling_half(slot, core), dst_ref=coupling_half(slot, core), send_sem=p_send.at[slot],
            recv_sem=p_recv.at[slot], device_id={"rhs": me + 1 - 2 * core}, device_id_type=pl.DeviceIdType.MESH,
        )

    def root_copy(part):
        if part < 3:
            src, dst = diag.at[0, part], d_in.at[part]
        else:
            src, dst = links.at[0, 2 * N : 2 * N + 8, :], d_rhs
        return pltpu.make_async_remote_copy(
            src_ref=src, dst_ref=dst, send_sem=d_send.at[part], recv_sem=d_recv.at[part],
            device_id={"tm": middle}, device_id_type=pl.DeviceIdType.MESH,
        )

    def message(t, blk, side, place, hop, part):
        slot = 1 - side
        if part < 3:
            src, dst, sem = t_out.at[blk, side, part], t_in.at[t, slot, part], t_recv.at[t, slot, part]
        elif part == 3:
            src, dst, sem = r_out.at[blk, side], r_in.at[t, slot], t_recv.at[t, slot, 3]
        else:
            dst = coupling_half(slot, core)
            src, sem = c_out.at[blk], a_recv.at[slot]
        return pltpu.make_async_remote_copy(
            src_ref=src, dst_ref=dst, send_sem=m_send.at[blk, place, part], recv_sem=sem,
            device_id={"tm": pos + hop * (2 * side - 1)}, device_id_type=pl.DeviceIdType.MESH,
        )

    def exists(there):
        return (there >= 0) & (there < width)

    def next_odd_side(t, step):
        quarter = jnp.where(t == 0, 2 * pos + 1, pos // step) % 4
        return jnp.where(quarter == 1, 1, 0)

    def absorb(t, part):
        def take(slot):
            arrival = message(t - 1, 0, 1 - slot, 0, 1, part)
            arrival.wait_recv()
            if part < 3:
                diag[0, part] = diag[0, part] - t_in[t - 1, slot, part]
            else:
                links[0, 2 * N : 2 * N + 8, :] = links[0, 2 * N : 2 * N + 8, :] - r_in[t - 1, slot]

        @pl.when(pos > 0)
        def _():
            take(0)

        @pl.when(t >= 2)
        def _():
            take(1)

    def products(t, blk, step):
        side_o = next_odd_side(t, step)
        hop = jnp.where(t == 0, 1, step)
        last = t == levels
        y_rows = slice(2 * N, 2 * N + 8)

        def gains(start, size):
            rows = pl.ds(start, size)
            gain[blk, rows, :] = nn(links[blk, rows, :], full[...])

        for place in range(2):
            side = side_o if place == 0 else 1 - side_o
            at = pl.multiple_of(side * N, N)
            other_at = pl.multiple_of((1 - side) * N, N)
            there = pos + hop * (2 * side - 1)
            local = (t == 0) & (side == 0)
            remote = exists(there) & jnp.logical_not(local | last)

            def send(part):
                @pl.when(remote)
                def _():
                    message(t, blk, side, place, hop, part).start()

            def give():
                for part, (r, c) in enumerate(((0, 0), (1, 0), (1, 1))):
                    left = pl.ds(pl.multiple_of(at + r * H, H), H)
                    right = pl.ds(pl.multiple_of(at + c * H, H), H)
                    if part < 2:
                        gains(pl.multiple_of(at + r * H, H), H)
                    t_out[blk, side, part] = nt(gain[blk, left, :], links[blk, right, :])
                    send(part)
                if place == 0:
                    gains(2 * N, 8)
                mat = links[blk, pl.ds(at, N), :]
                r_out[blk, side] = nt(gain[blk, y_rows, :], mat)
                send(3)

                if place == 0:
                    own = pl.ds(pl.multiple_of(other_at + core * H, H), H)
                    gains(pl.multiple_of(other_at + core * H, H), H)
                    c_out[blk] = -nt(gain[blk, own, :], mat)
                    send(4)

                @pl.when(local)
                def _():
                    for part in range(3):
                        diag[0, part] = diag[0, part] - t_out[blk, side, part]
                    links[0, y_rows, :] = links[0, y_rows, :] - r_out[blk, side]
                    if place == 0:
                        gains(other_at, N)
                        links[0, N : 2 * N, :] = -nt(gain[blk, pl.ds(other_at, N), :], mat)

            if place == 0:
                pl.when(jnp.logical_not(last))(give)

                @pl.when(last)
                def _():
                    gains(2 * N, 8)
            else:
                give()

        @pl.when(last)
        def _():
            for part in range(4):
                root_copy(part).wait_recv()
            for part in range(3):
                diag[0, part] = d_in[part] - t_out[blk, 0, part]
            d_rhs[...] = d_rhs[...] - r_out[blk, 0]

    def wait_sent(t, blk, step):
        side_o = next_odd_side(t, step)
        hop = jnp.where(t == 0, 1, step)
        for place in range(2):
            side = side_o if place == 0 else 1 - side_o
            there = pos + hop * (2 * side - 1)
            remote = exists(there) & jnp.logical_not(((t == 0) & (side == 0)) | (t == levels))

            @pl.when(remote)
            def _(side=side, place=place):
                for part in range(5 - place):
                    message(t, blk, side, place, hop, part).wait_send()

    def each_map(level, act):
        for sign in (-1, 1) if level > 0 else (-1,):
            there = pos + sign * (2**level // 2 if level > 0 else 1)
            act(
                pltpu.make_async_remote_copy(
                    src_ref=gain.at[0], dst_ref=map_o if level > 0 else map_n,
                    send_sem=g_send.at[0 if sign < 0 else 1], recv_sem=g_recv.at[0 if level > 0 else 1],
                    device_id={"tm": there}, device_id_type=pl.DeviceIdType.MESH,
                )
            )

    def eliminate(t, step):
        blk = jnp.where(t == 0, 1, 0)
        active = (t >= 1) & (t <= levels) & (pos % step == 0)
        odd = active & (pos // step % 2 == 1)
        root = (t == levels + 1) & (pos == middle)
        invert = (t == 0) | odd | root

        def part_of(h, carry):
            @pl.when((t == 0) & (h == 1))
            def _():
                local_block(0)

            @pl.when(active & (h == 0))
            def _():
                absorb(t, 0)

            @pl.when(active & (h == 1))
            def _():
                for part in (1, 2, 3):
                    absorb(t, part)

            @pl.when(invert & (h == 1))
            def _():
                half[...] = -nn(diag[blk, 1], diag[blk, 0])
                diag[blk, 2] = diag[blk, 2] - nt(half[...], diag[blk, 1])

            @pl.when(invert)
            def _():
                sweep(diag.at[blk, 2 * h])

            return carry

        lax.fori_loop(0, 2, part_of, 0)

        @pl.when((t == levels) & (pos == 0))
        def _():
            for part in range(4):
                root_copy(part).start()

        def each_coupling(act):
            @pl.when(odd)
            def _():
                act(0)

                @pl.when(t >= 2)
                def _():
                    act(1)

        def hand_on(slot):
            message(t - 1, 0, 1 - slot, 0, 1, 4).wait_recv()
            pair_copy(slot).start()

        each_coupling(hand_on)

        @pl.when(invert)
        def _():
            lower = nn(diag[blk, 2], half[...])
            upper = lower.T
            full[H:, H:] = -diag[blk, 2]
            full[H:, :H] = lower
            full[:H, H:] = upper
            full[:H, :H] = -diag[blk, 0] - nn(upper, half[...])

        each_coupling(lambda slot: pair_copy(slot).wait_recv())

        @pl.when(odd | (t == 0))
        def _():
            products(t, blk, step)

        for level in tops:
            @pl.when(odd & (t == level + 1))
            def _(level=level):
                each_map(level, lambda copy: copy.start())

        @pl.when(odd)
        def _():
            wait_sent(t, blk, step)

        each_coupling(lambda slot: pair_copy(slot).wait_send())

        @pl.when(root)
        def _():
            x_root[...] = nn(d_rhs[...], full[...])

        return jnp.where(t == 0, 1, 2 * step)

    lax.fori_loop(0, levels + 2, eliminate, jnp.int32(1))

    def x_copy(src, there, slot, index):
        return pltpu.make_async_remote_copy(
            src_ref=src, dst_ref=x_in.at[slot], send_sem=x_send.at[index], recv_sem=x_recv.at[slot],
            device_id={"tm": there}, device_id_type=pl.DeviceIdType.MESH,
        )

    def wait_for(slot):
        x_copy(x_own, pos, slot, 0).wait_recv()

    def group_targets(at, top):
        if top == 0:
            return [(at + 1, 0), (at - 1, 1), (at - 2, 3)]
        reach = 2**top
        near = [(at + reach, 0), (at - reach, 1)]
        half_reach = reach // 2
        return near + [
            (at + half_reach, 0), (at - half_reach, 1), (at + 3 * half_reach, 2), (at - 3 * half_reach, 2),
        ]

    def each_target(src, at, level, base, act):
        index = base
        for top in tops:
            if top <= level:
                for there, slot in group_targets(at, top):
                    @pl.when(exists(there))
                    def _(there=there, slot=slot, index=index):
                        act(x_copy(src, there, slot, index))
                    index += 1

    def start(copy):
        copy.start()

    def sent(copy):
        copy.wait_send()

    def term(x, of, side):
        return nn(x, of[pl.ds(pl.multiple_of(side * N, N), N), :])

    own_map = gain.at[0]

    def root_targets(act):
        each_target(x_root, 0, levels - 2, 0, act)

    def home_copy():
        return pltpu.make_async_remote_copy(
            src_ref=x_root, dst_ref=x_in.at[0], send_sem=z_send, recv_sem=x_recv.at[0],
            device_id={"tm": 0}, device_id_type=pl.DeviceIdType.MESH,
        )

    @pl.when(pos == middle)
    def _():
        root_targets(start)
        home_copy().start()
        x_own[...] = gain[0, 2 * N : 2 * N + 8, :] - nn(x_root[...], gain[0, 0:N, :])
        each_target(x_own, middle, levels - 2, 24, start)

    @pl.when(pos == 0)
    def _():
        wait_for(0)
        x_own[...] = x_in[0]

    for level in reversed(range(levels - 1)):
        step = 2**level
        top = [t for t in tops if level in (t, t - 1)][0]

        @pl.when(pos % (2 * step) == step)
        def _(level=level, step=step, top=top):
            upper = pos + step < width
            x_own[...] = gain[0, 2 * N : 2 * N + 8, :]
            if level == top:
                wait_for(0)
                x_own[...] = x_own[...] - term(x_in[0], own_map, 0)

                @pl.when(upper)
                def _():
                    wait_for(1)
                    x_own[...] = x_own[...] - term(x_in[1], own_map, 1)
            else:
                side_o = next_odd_side(1, step)
                side_e = 1 - side_o
                each_end = ((side_e, side_e, exists(pos + step * (2 * side_e - 1))),
                            (side_o, 2, exists(pos + 3 * step * (2 * side_o - 1))))
                pltpu.make_async_remote_copy(
                    src_ref=own_map, dst_ref=map_o, send_sem=g_send.at[0], recv_sem=g_recv.at[0],
                    device_id={"tm": pos}, device_id_type=pl.DeviceIdType.MESH,
                ).wait_recv()
                x_o[...] = map_o[2 * N : 2 * N + 8, :]
                for side, slot, there in each_end:
                    @pl.when(there)
                    def _(side=side, slot=slot):
                        wait_for(slot)
                        x_o[...] = x_o[...] - term(x_in[slot], map_o, side)

                @pl.when(exists(pos + step * (2 * side_e - 1)))
                def _():
                    x_own[...] = x_own[...] - term(x_in[side_e], own_map, side_e)

                x_own[...] = x_own[...] - term(x_o[...], own_map, side_o)
            if level > 0:
                each_target(x_own, pos, top - 1 if level == top else top - 2, 0, start)

    out[:, 0, :] = x_own[...]
    out[:, 1, :] = gain[1, 2 * N : 2 * N + 8, :] - nn(x_own[...], gain[1, 0:N, :])

    @pl.when(pos % 2 == 0)
    def _():
        pltpu.make_async_remote_copy(
            src_ref=own_map, dst_ref=map_n, send_sem=g_send.at[0], recv_sem=g_recv.at[1],
            device_id={"tm": pos}, device_id_type=pl.DeviceIdType.MESH,
        ).wait_recv()
        x_o[...] = map_n[2 * N : 2 * N + 8, :] - term(x_own[...], map_n, 0)

        @pl.when(pos + 2 < width)
        def _():
            wait_for(3)
            x_o[...] = x_o[...] - term(x_in[3], map_n, 1)

        out[:, 1, :] = out[:, 1, :] - nn(x_o[...], gain[1, N : 2 * N, :])

    @pl.when((pos % 2 == 1) & (pos < width - 1))
    def _():
        out[:, 1, :] = out[:, 1, :] - nn(x_in[1], gain[1, N : 2 * N, :])

    wait_sent(jnp.int32(0), 1, jnp.int32(1))

    @pl.when(pos == 0)
    def _():
        for part in range(4):
            root_copy(part).wait_send()

    @pl.when(pos == middle)
    def _():
        root_targets(sent)
        home_copy().wait_send()
        each_target(x_own, middle, levels - 2, 24, sent)

    for level in range(levels - 1):
        top = [t for t in tops if level in (t, t - 1)][0]

        @pl.when(pos % (2 * 2**level) == 2**level)
        def _(level=level, top=top):
            if level == top:
                each_map(level, sent)
            if level > 0:
                each_target(x_own, pos, top - 1 if level == top else top - 2, 0, sent)


def per_device(jacobians, damping, right_sides):
    width = lax.axis_size("tm")
    peers = lax.axis_size("rhs")
    levels = width.bit_length() - 1
    vmem = pl.BlockSpec(memory_space=pltpu.VMEM)
    return pl.pallas_call(
        functools.partial(kernel, width, peers, levels),
        out_shape=jax.ShapeDtypeStruct(right_sides.shape, F32),
        in_specs=[pl.BlockSpec(memory_space=pl.ANY)] * 3,
        out_specs=vmem,
        scratch_shapes=[
            pltpu.VMEM((2, N, N), jnp.bfloat16),
            pltpu.VMEM(damping.shape, F32),
            pltpu.VMEM(right_sides.shape, F32),
            pltpu.VMEM((2, 3, H, H), F32),
            pltpu.VMEM((2, 2 * N + 8, N), F32),
            pltpu.VMEM((H, H), F32),
            pltpu.VMEM((N, N), F32),
            pltpu.VMEM((2, 2 * N + 8, N), F32),
            pltpu.VMEM((2, 2, 3, H, H), F32),
            pltpu.VMEM((2, 2, 8, N), F32),
            pltpu.VMEM((2, H, N), F32),
            pltpu.VMEM((levels, 2, 3, H, H), F32),
            pltpu.VMEM((levels, 2, 8, N), F32),
            pltpu.VMEM((3, H, H), F32),
            pltpu.VMEM((8, N), F32),
            pltpu.VMEM((2 * N + 8, N), F32),
            pltpu.VMEM((2 * N + 8, N), F32),
            pltpu.VMEM((8, N), F32),
            pltpu.VMEM((8, N), F32),
            pltpu.VMEM((8, N), F32),
            pltpu.VMEM((4, 8, N), F32),
            pltpu.SemaphoreType.DMA((3,)),
            pltpu.SemaphoreType.DMA((2, peers - 1)),
            pltpu.SemaphoreType.DMA((2, peers - 1)),
            pltpu.SemaphoreType.DMA((2, 2, 5)),
            pltpu.SemaphoreType.DMA((levels, 2, 4)),
            pltpu.SemaphoreType.DMA((2,)),
            pltpu.SemaphoreType.DMA((2,)),
            pltpu.SemaphoreType.DMA((2,)),
            pltpu.SemaphoreType.DMA((4,)),
            pltpu.SemaphoreType.DMA((4,)),
            pltpu.SemaphoreType.DMA((2,)),
            pltpu.SemaphoreType.DMA((2,)),
            pltpu.SemaphoreType.DMA(()),
            pltpu.SemaphoreType.DMA((48,)),
            pltpu.SemaphoreType.DMA((4,)),
        ],
        compiler_params=pltpu.CompilerParams(
            collective_id=0, has_side_effects=True, vmem_limit_bytes=32 * 1024 * 1024
        ),
    )(jacobians, damping, right_sides)


def solution(mesh):
    in_specs = (P("tm", "rhs", None), P("tm", None), P("rhs", "tm", None))
    return jax.shard_map(
        per_device, mesh=mesh, in_specs=in_specs, out_specs=P("rhs", "tm", None), check_vma=False
    )
```

```python
import functools

import jax
import jax.numpy as jnp
from jax import lax
from jax.experimental import pallas as pl
from jax.experimental.pallas import tpu as pltpu
from jax.sharding import PartitionSpec as P

HIGHEST = lax.Precision.HIGHEST
F32 = jnp.float32
N = 256
H = 128


def nn(a, b):
    return lax.dot_general(a, b, (((1,), (0,)), ((), ())), precision=HIGHEST, preferred_element_type=F32)


def nt(a, b):
    return lax.dot_general(a, b, (((1,), (1,)), ((), ())), precision=HIGHEST, preferred_element_type=F32)


def in_parts(x, count):
    parts = []
    for _ in range(count):
        parts.append(x.astype(jnp.bfloat16))
        x = x - parts[-1].astype(F32)
    return parts


def joined(a, b, order, axis):
    left = jnp.concatenate([a[i] for i, _ in order], axis=1)
    right = jnp.concatenate([b[j] for _, j in order], axis=axis)
    return lax.dot_general(left, right, (((1,), (axis,)), ((), ())), preferred_element_type=F32)


SIX = ((2, 0), (0, 2), (1, 1), (1, 0), (0, 1), (0, 0))


def nn6(a, b):
    return joined(in_parts(a, 3), in_parts(b, 3), SIX, 0)


def nt6(a, b):
    return joined(in_parts(a, 3), in_parts(b, 3), SIX, 1)


def thrice(a, b):
    return joined(in_parts(a, 2), in_parts(b, 2), ((1, 0), (0, 1), (0, 0)), 0)


def spread(x):
    return jnp.broadcast_to(x, (8, 128))


def tree_sum(terms):
    while len(terms) > 1:
        terms = [terms[i] + terms[i + 1] for i in range(0, len(terms), 2)]
    return terms[0]


def sweep8(cols, sub):
    for a in range(0, 8, 2):
        b = a + 1
        row_a = [spread(c[a : a + 1, :]) for c in cols]
        row_b = [spread(c[b : b + 1, :]) for c in cols]
        aa, ab, bb = row_a[a], row_a[b], row_b[b]
        det = aa * bb - ab * ab
        guess = pl.reciprocal(det, approx=True)
        mend = 2.0 - det * guess
        is_a, is_b = sub == a, sub == b
        part_a = jnp.where(is_a, -bb, jnp.where(is_b, ab, bb * cols[a] - ab * cols[b])) * guess
        part_b = jnp.where(is_a, ab, jnp.where(is_b, -aa, aa * cols[b] - ab * cols[a])) * guess
        new = []
        for j in range(8):
            if j == a:
                new.append(part_a * mend)
            elif j == b:
                new.append(part_b * mend)
            else:
                kept = jnp.where(is_a | is_b, 0.0, cols[j])
                new.append(kept - (part_a * row_a[j] + part_b * row_b[j]) * mend)
        cols = new
    return cols


def sweep(ref):
    lane = lax.broadcasted_iota(jnp.int32, (8, 128), 1)
    sub = lax.broadcasted_iota(jnp.int32, (8, 128), 0)
    rows = [ref[8 * g : 8 * g + 8, :] for g in range(16)]
    for start in (0, 8):
        panel = range(start, start + 8)
        for w in panel:
            k0 = 8 * w
            inside = (lane >= k0) & (lane < k0 + 8)
            pivots = rows[w]
            cols = sweep8([spread(pivots[:, k0 + j : k0 + j + 1]) + 0.0 for j in range(8)], sub)
            terms = []
            for j in range(8):
                row = jnp.where(inside, jnp.where(lane == k0 + j, -1.0, 0.0), spread(pivots[j : j + 1, :]))
                terms.append(cols[j] * row)
            swept = tree_sum(terms)
            minus = [spread(swept[j : j + 1, :]) for j in range(8)]
            for g in list(range(w + 1, start + 8)) + list(range(start, w)):
                terms = [spread(rows[g][:, k0 + j : k0 + j + 1]) * minus[j] for j in range(8)]
                rows[g] = jnp.where(inside, 0.0, rows[g]) + tree_sum(terms)
            rows[w] = -swept
        others = range(8 - start, 16 - start)
        zero = jnp.zeros((8, 128), F32)
        far = jnp.concatenate([rows[g] for g in others], axis=0)
        near = jnp.concatenate([rows[g] if g in panel else zero for g in range(16)], axis=0)
        change = nn(far, near)
        inside = (lane >= 8 * start) & (lane < 8 * start + 64)
        for index, g in enumerate(others):
            rows[g] = jnp.where(inside, 0.0, rows[g]) - change[8 * index : 8 * index + 8, :]
    for g in range(16):
        ref[8 * g : 8 * g + 8, :] = rows[g]


def kernel(
    width, peers, levels,
    jac, damp, rhs, out,
    whole, damp_in, rhs_in, diag, links, half, full, gain, t_out, r_out, c_out, t_in, r_in,
    d_in, d_rhs, map_o, map_n, x_root, x_own, x_o, x_in,
    i_sem, j_send, j_recv, m_send, t_recv, a_recv, p_send, p_recv, d_send, d_recv, token, g_send, g_recv, z_send, x_send, x_recv,
):
    pos = lax.axis_index("tm")
    me = lax.axis_index("rhs")
    middle = width // 2
    tops = list(range(levels - 2, -1, -2))
    core = me % 2

    depth = jac.shape[1]
    mine = pl.ds(pl.multiple_of(me * depth, depth), depth)
    loads = [
        pltpu.make_async_copy(jac, whole.at[:, mine, :], i_sem.at[0]),
        pltpu.make_async_copy(damp, damp_in, i_sem.at[1]),
        pltpu.make_async_copy(rhs, rhs_in, i_sem.at[2]),
    ]
    for load in loads:
        load.start()

    barrier = pltpu.get_barrier_semaphore()
    count = peers - 1
    for d in range(1, peers):
        pl.semaphore_signal(barrier, inc=1, device_id={"rhs": (me + d) % peers}, device_id_type=pl.DeviceIdType.MESH)
    for sign in (-1, 1):
        there = pos + sign
        partner = (there >= 0) & (there < width)
        count = count + partner.astype(jnp.int32)

        @pl.when(partner)
        def _(there=there):
            pl.semaphore_signal(barrier, inc=1, device_id={"tm": there}, device_id_type=pl.DeviceIdType.MESH)
    pl.semaphore_wait(barrier, count)

    def row_copy(k, d):
        return pltpu.make_async_remote_copy(
            src_ref=jac.at[k], dst_ref=whole.at[k, mine, :], send_sem=j_send.at[k, d - 1], recv_sem=j_recv.at[k, d - 1],
            device_id={"rhs": (me + d) % peers}, device_id_type=pl.DeviceIdType.MESH,
        )

    for k in (1, 0):
        for d in range(1, peers):
            row_copy(k, d).start()
    for load in loads:
        load.wait()

    def local_block(k):
        for d in range(1, peers):
            row_copy(k, d).wait()
        on_diag = lax.broadcasted_iota(jnp.int32, (N, N), 0) == lax.broadcasted_iota(jnp.int32, (N, N), 1)
        block = lax.dot_general(whole[k], whole[k], (((0,), (0,)), ((), ())), preferred_element_type=F32)
        extra = damp_in[k : k + 1, :] + (jnp.where(pos > 0, 1.0, 0.0).astype(F32) if k == 0 else 1.0)
        block = block + jnp.where(on_diag, jnp.broadcast_to(extra, (N, N)), 0.0)
        diag[k, 0] = block[:H, :H]
        diag[k, 1] = block[H:, :H]
        diag[k, 2] = block[H:, H:]
        links[k, 2 * N : 2 * N + 8, :] = rhs_in[:, k, :]
        if k == 0:
            links[1, 0:N, :] = -whole[0].astype(F32).T
        else:
            last = jnp.where(pos < width - 1, 1.0, 0.0).astype(F32)
            links[1, N : 2 * N, :] = -whole[1].astype(F32) * last

    local_block(1)

    def coupling_half(slot, which):
        return links.at[0, pl.ds(pl.multiple_of(slot * N + which * H, H), H), :]

    def pair_copy(slot):
        return pltpu.make_async_remote_copy(
            src_ref=coupling_half(slot, core), dst_ref=coupling_half(slot, core), send_sem=p_send.at[slot],
            recv_sem=p_recv.at[slot], device_id={"rhs": me + 1 - 2 * core}, device_id_type=pl.DeviceIdType.MESH,
        )

    def root_copy(part):
        if part < 3:
            src, dst = diag.at[0, part], d_in.at[part]
        else:
            src, dst = links.at[0, 2 * N : 2 * N + 8, :], d_rhs
        return pltpu.make_async_remote_copy(
            src_ref=src, dst_ref=dst, send_sem=d_send.at[part], recv_sem=d_recv.at[part],
            device_id={"tm": middle}, device_id_type=pl.DeviceIdType.MESH,
        )

    def message(t, blk, side, place, hop, part):
        slot = 1 - side
        past = (t == levels - 1) & (pos == middle // 2) & (side == 0)
        at, cell = jnp.where(past, 0, t), jnp.where(past, 1, slot)
        if part < 3:
            src, dst, sem = t_out.at[blk, side, part], t_in.at[at, cell, part], t_recv.at[at, cell, part]
        elif part == 3:
            src, dst, sem = r_out.at[blk, side], r_in.at[at, cell], t_recv.at[at, cell, 3]
        else:
            dst = coupling_half(slot, core)
            src, sem = c_out.at[blk], a_recv.at[slot]
        return pltpu.make_async_remote_copy(
            src_ref=src, dst_ref=dst, send_sem=m_send.at[blk, place, part], recv_sem=sem,
            device_id={"tm": jnp.where(past, middle, pos + hop * (2 * side - 1))}, device_id_type=pl.DeviceIdType.MESH,
        )

    def straight(part):
        dst = t_in.at[0, 1, part] if part < 3 else r_in.at[0, 1]
        return pltpu.make_async_remote_copy(
            src_ref=dst, dst_ref=dst, send_sem=m_send.at[0, 0, part], recv_sem=t_recv.at[0, 1, part],
            device_id={"tm": pos}, device_id_type=pl.DeviceIdType.MESH,
        )

    def exists(there):
        return (there >= 0) & (there < width)

    def next_odd_side(t, step):
        quarter = jnp.where(t == 0, 2 * pos + 1, pos // step) % 4
        return jnp.where(quarter == 1, 1, 0)

    def absorb(t, part):
        def take(slot):
            arrival = message(t - 1, 0, 1 - slot, 0, 1, part)
            arrival.wait_recv()
            if part < 3:
                diag[0, part] = diag[0, part] - t_in[t - 1, slot, part]
            else:
                links[0, 2 * N : 2 * N + 8, :] = links[0, 2 * N : 2 * N + 8, :] - r_in[t - 1, slot]

        @pl.when(pos > 0)
        def _():
            take(0)

        @pl.when(t >= 2)
        def _():
            take(1)

    def products(t, blk, step):
        side_o = next_odd_side(t, step)
        hop = jnp.where(t == 0, 1, step)
        last = t == levels
        y_rows = slice(2 * N, 2 * N + 8)

        def gains(start, size):
            rows = pl.ds(start, size)
            gain[blk, rows, :] = nn(links[blk, rows, :], full[...])

        for place in range(2):
            side = side_o if place == 0 else 1 - side_o
            at = pl.multiple_of(side * N, N)
            other_at = pl.multiple_of((1 - side) * N, N)
            there = pos + hop * (2 * side - 1)
            local = (t == 0) & (side == 0)
            remote = exists(there) & jnp.logical_not(local | last)

            def send(part):
                @pl.when(remote)
                def _():
                    message(t, blk, side, place, hop, part).start()

            def give():
                for part, (r, c) in enumerate(((0, 0), (1, 0), (1, 1))):
                    left = pl.ds(pl.multiple_of(at + r * H, H), H)
                    right = pl.ds(pl.multiple_of(at + c * H, H), H)
                    if part < 2:
                        gains(pl.multiple_of(at + r * H, H), H)
                    t_out[blk, side, part] = nt(gain[blk, left, :], links[blk, right, :])
                    send(part)
                if place == 0:
                    gains(2 * N, 8)
                mat = links[blk, pl.ds(at, N), :]
                r_out[blk, side] = nt(gain[blk, y_rows, :], mat)
                send(3)

                if place == 0:
                    own = pl.ds(pl.multiple_of(other_at + core * H, H), H)
                    gains(pl.multiple_of(other_at + core * H, H), H)
                    c_out[blk] = -nt(gain[blk, own, :], mat)
                    send(4)

                @pl.when(local)
                def _():
                    for part in range(3):
                        diag[0, part] = diag[0, part] - t_out[blk, side, part]
                    links[0, y_rows, :] = links[0, y_rows, :] - r_out[blk, side]
                    if place == 0:
                        gains(other_at, N)
                        links[0, N : 2 * N, :] = -nt(gain[blk, pl.ds(other_at, N), :], mat)

            if place == 0:
                pl.when(jnp.logical_not(last))(give)

                @pl.when(last)
                def _():
                    gains(2 * N, 8)
            else:
                give()

        @pl.when(last)
        def _():
            for part in range(4):
                root_copy(part).wait_recv()
                straight(part).wait_recv()
            for part in range(3):
                diag[0, part] = d_in[part] - t_in[0, 1, part] - t_out[blk, 0, part]
            d_rhs[...] = d_rhs[...] - r_in[0, 1] - r_out[blk, 0]

    def wait_sent(t, blk, step):
        side_o = next_odd_side(t, step)
        hop = jnp.where(t == 0, 1, step)
        for place in range(2):
            side = side_o if place == 0 else 1 - side_o
            there = pos + hop * (2 * side - 1)
            remote = exists(there) & jnp.logical_not(((t == 0) & (side == 0)) | (t == levels))

            @pl.when(remote)
            def _(side=side, place=place):
                for part in range(5 - place):
                    message(t, blk, side, place, hop, part).wait_send()

    def each_map(level, act):
        for sign in (-1, 1) if level > 0 else (-1,):
            there = pos + sign * (2**level // 2 if level > 0 else 1)
            act(
                pltpu.make_async_remote_copy(
                    src_ref=gain.at[0], dst_ref=map_o if level > 0 else map_n,
                    send_sem=g_send.at[0 if sign < 0 else 1], recv_sem=g_recv.at[0 if level > 0 else 1],
                    device_id={"tm": there}, device_id_type=pl.DeviceIdType.MESH,
                )
            )

    def eliminate(t, step):
        blk = jnp.where(t == 0, 1, 0)
        active = (t >= 1) & (t <= levels) & (pos % step == 0) & ((t < levels) | (pos > 0))
        odd = active & (pos // step % 2 == 1)
        root = (t == levels + 1) & (pos == middle)
        invert = (t == 0) | odd | root

        def part_of(h, carry):
            @pl.when((t == 0) & (h == 1))
            def _():
                local_block(0)

            @pl.when(active & (h == 0))
            def _():
                absorb(t, 0)

            @pl.when(active & (h == 0) & (t == levels - 1) & (pos == middle // 2))
            def _():
                pl.semaphore_signal(token, inc=1, device_id={"tm": 0}, device_id_type=pl.DeviceIdType.MESH)

            @pl.when(active & (h == 1))
            def _():
                for part in (1, 2, 3):
                    absorb(t, part)

            @pl.when(invert & (h == 1))
            def _():
                half[...] = -nn6(diag[blk, 1], diag[blk, 0])
                diag[blk, 2] = diag[blk, 2] - nt6(half[...], diag[blk, 1])

            @pl.when(invert)
            def _():
                sweep(diag.at[blk, 2 * h])

            return carry

        lax.fori_loop(0, 2, part_of, 0)

        @pl.when((t == levels - 1) & (pos == 0))
        def _():
            pl.semaphore_wait(token, 1)
            for part in range(4):
                root_copy(part).start()

        def each_coupling(act):
            @pl.when(odd)
            def _():
                act(0)

                @pl.when(t >= 2)
                def _():
                    act(1)

        def hand_on(slot):
            message(t - 1, 0, 1 - slot, 0, 1, 4).wait_recv()
            pair_copy(slot).start()

        each_coupling(hand_on)

        @pl.when(invert)
        def _():
            lower = nn6(diag[blk, 2], half[...])
            upper = lower.T
            full[H:, H:] = -diag[blk, 2]
            full[H:, :H] = lower
            full[:H, H:] = upper
            full[:H, :H] = -diag[blk, 0] - nn6(upper, half[...])

        each_coupling(lambda slot: pair_copy(slot).wait_recv())

        @pl.when(odd | (t == 0))
        def _():
            products(t, blk, step)

        for level in tops:
            @pl.when(odd & (t == level + 1))
            def _(level=level):
                each_map(level, lambda copy: copy.start())

        @pl.when(odd)
        def _():
            wait_sent(t, blk, step)

        each_coupling(lambda slot: pair_copy(slot).wait_send())

        @pl.when(root)
        def _():
            x_root[...] = nn(d_rhs[...], full[...])

        return jnp.where(t == 0, 1, 2 * step)

    lax.fori_loop(0, levels + 2, eliminate, jnp.int32(1))

    def x_copy(src, there, slot, index):
        return pltpu.make_async_remote_copy(
            src_ref=src, dst_ref=x_in.at[slot], send_sem=x_send.at[index], recv_sem=x_recv.at[slot],
            device_id={"tm": there}, device_id_type=pl.DeviceIdType.MESH,
        )

    def wait_for(slot):
        x_copy(x_own, pos, slot, 0).wait_recv()

    def group_targets(at, top):
        if top == 0:
            return [(at + 1, 0), (at - 1, 1), (at - 2, 3)]
        reach = 2**top
        near = [(at + reach, 0), (at - reach, 1)]
        half_reach = reach // 2
        return near + [
            (at + half_reach, 0), (at - half_reach, 1), (at + 3 * half_reach, 2), (at - 3 * half_reach, 2),
        ]

    def each_target(src, at, group_tops, base, act):
        for top in group_tops:
            index = base + 6 * tops.index(top)
            for there, slot in group_targets(at, top):
                @pl.when(exists(there))
                def _(there=there, slot=slot, index=index):
                    act(x_copy(src, there, slot, index))
                index += 1

    def below(level):
        return [top for top in tops if top < level]

    def start(copy):
        copy.start()

    def sent(copy):
        copy.wait_send()

    def take(slot, there):
        @pl.when(there)
        def _():
            wait_for(slot)

        @pl.when(jnp.logical_not(there))
        def _():
            x_in[slot] = jnp.zeros((8, N), F32)

    def solved(of, lower, upper):
        ends = jnp.concatenate([lower, upper], axis=1)
        return of[2 * N : 2 * N + 8, :] - thrice(ends, of[0 : 2 * N, :])

    own_map = gain.at[0]

    def home_copy():
        return pltpu.make_async_remote_copy(
            src_ref=x_root, dst_ref=x_in.at[0], send_sem=z_send, recv_sem=x_recv.at[0],
            device_id={"tm": 0}, device_id_type=pl.DeviceIdType.MESH,
        )

    @pl.when(pos == middle)
    def _():
        each_target(x_root, 0, tops[:1], 0, start)
        x_own[...] = gain[0, 2 * N : 2 * N + 8, :] - thrice(x_root[...], gain[0, 0:N, :])
        each_target(x_own, middle, tops[:1], 24, start)
        each_target(x_root, 0, tops[1:], 0, start)
        each_target(x_own, middle, tops[1:], 24, start)
        home_copy().start()

    @pl.when(pos == 0)
    def _():
        wait_for(0)
        x_own[...] = x_in[0]

    for level in reversed(range(levels - 1)):
        step = 2**level
        top = [t for t in tops if level in (t, t - 1)][0]

        @pl.when(pos % (2 * step) == step)
        def _(level=level, step=step, top=top):
            if level == top:
                take(0, pos >= 0)
                take(1, pos + step < width)
                x_own[...] = solved(own_map, x_in[0], x_in[1])
            else:
                side_o = next_odd_side(1, step)
                side_e = 1 - side_o
                pltpu.make_async_remote_copy(
                    src_ref=own_map, dst_ref=map_o, send_sem=g_send.at[0], recv_sem=g_recv.at[0],
                    device_id={"tm": pos}, device_id_type=pl.DeviceIdType.MESH,
                ).wait_recv()
                take(side_e, exists(pos + step * (2 * side_e - 1)))
                take(2, exists(pos + 3 * step * (2 * side_o - 1)))
                near, far = x_in[side_e], x_in[2]
                flip = side_e == 1
                between = solved(map_o, jnp.where(flip, far, near), jnp.where(flip, near, far))
                x_own[...] = solved(own_map, jnp.where(flip, between, near), jnp.where(flip, near, between))
            if level > 0:
                each_target(x_own, pos, below(level if level == top else top), 0, start)

    out[:, 0, :] = x_own[...]

    @pl.when(pos % 2 == 0)
    def _():
        pltpu.make_async_remote_copy(
            src_ref=own_map, dst_ref=map_n, send_sem=g_send.at[0], recv_sem=g_recv.at[1],
            device_id={"tm": pos}, device_id_type=pl.DeviceIdType.MESH,
        ).wait_recv()
        take(3, pos + 2 < width)
        out[:, 1, :] = solved(gain.at[1], x_own[...], solved(map_n, x_own[...], x_in[3]))

    @pl.when(pos % 2 == 1)
    def _():
        out[:, 1, :] = solved(gain.at[1], x_own[...], x_in[1])

    wait_sent(jnp.int32(0), 1, jnp.int32(1))

    @pl.when(pos == 0)
    def _():
        for part in range(4):
            root_copy(part).wait_send()

    @pl.when(pos == middle)
    def _():
        each_target(x_root, 0, tops, 0, sent)
        each_target(x_own, middle, tops, 24, sent)
        home_copy().wait_send()

    for level in range(levels - 1):
        top = [t for t in tops if level in (t, t - 1)][0]

        @pl.when(pos % (2 * 2**level) == 2**level)
        def _(level=level, top=top):
            if level == top:
                each_map(level, sent)
            if level > 0:
                each_target(x_own, pos, below(level if level == top else top), 0, sent)


def per_device(jacobians, damping, right_sides):
    width = lax.axis_size("tm")
    peers = lax.axis_size("rhs")
    levels = width.bit_length() - 1
    vmem = pl.BlockSpec(memory_space=pltpu.VMEM)
    return pl.pallas_call(
        functools.partial(kernel, width, peers, levels),
        out_shape=jax.ShapeDtypeStruct(right_sides.shape, F32),
        in_specs=[pl.BlockSpec(memory_space=pl.ANY)] * 3,
        out_specs=vmem,
        scratch_shapes=[
            pltpu.VMEM((2, N, N), jnp.bfloat16),
            pltpu.VMEM(damping.shape, F32),
            pltpu.VMEM(right_sides.shape, F32),
            pltpu.VMEM((2, 3, H, H), F32),
            pltpu.VMEM((2, 2 * N + 8, N), F32),
            pltpu.VMEM((H, H), F32),
            pltpu.VMEM((N, N), F32),
            pltpu.VMEM((2, 2 * N + 8, N), F32),
            pltpu.VMEM((2, 2, 3, H, H), F32),
            pltpu.VMEM((2, 2, 8, N), F32),
            pltpu.VMEM((2, H, N), F32),
            pltpu.VMEM((levels, 2, 3, H, H), F32),
            pltpu.VMEM((levels, 2, 8, N), F32),
            pltpu.VMEM((3, H, H), F32),
            pltpu.VMEM((8, N), F32),
            pltpu.VMEM((2 * N + 8, N), F32),
            pltpu.VMEM((2 * N + 8, N), F32),
            pltpu.VMEM((8, N), F32),
            pltpu.VMEM((8, N), F32),
            pltpu.VMEM((8, N), F32),
            pltpu.VMEM((4, 8, N), F32),
            pltpu.SemaphoreType.DMA((3,)),
            pltpu.SemaphoreType.DMA((2, peers - 1)),
            pltpu.SemaphoreType.DMA((2, peers - 1)),
            pltpu.SemaphoreType.DMA((2, 2, 5)),
            pltpu.SemaphoreType.DMA((levels, 2, 4)),
            pltpu.SemaphoreType.DMA((2,)),
            pltpu.SemaphoreType.DMA((2,)),
            pltpu.SemaphoreType.DMA((2,)),
            pltpu.SemaphoreType.DMA((4,)),
            pltpu.SemaphoreType.DMA((4,)),
            pltpu.SemaphoreType.REGULAR,
            pltpu.SemaphoreType.DMA((2,)),
            pltpu.SemaphoreType.DMA((2,)),
            pltpu.SemaphoreType.DMA(()),
            pltpu.SemaphoreType.DMA((48,)),
            pltpu.SemaphoreType.DMA((4,)),
        ],
        compiler_params=pltpu.CompilerParams(
            collective_id=0, has_side_effects=True, vmem_limit_bytes=32 * 1024 * 1024
        ),
    )(jacobians, damping, right_sides)


def solution(mesh):
    in_specs = (P("tm", "rhs", None), P("tm", None), P("rhs", "tm", None))
    return jax.shard_map(
        per_device, mesh=mesh, in_specs=in_specs, out_specs=P("rhs", "tm", None), check_vma=False
    )
```

```python
import functools

import jax
import jax.numpy as jnp
from jax import lax
from jax.experimental import pallas as pl
from jax.experimental.pallas import tpu as pltpu
from jax.sharding import PartitionSpec as P

HIGHEST = lax.Precision.HIGHEST
F32 = jnp.float32
N = 256
H = 128


def nn(a, b):
    return lax.dot_general(a, b, (((1,), (0,)), ((), ())), precision=HIGHEST, preferred_element_type=F32)


def nt(a, b):
    return lax.dot_general(a, b, (((1,), (1,)), ((), ())), precision=HIGHEST, preferred_element_type=F32)


def in_parts(x, count):
    parts = []
    for _ in range(count):
        parts.append(x.astype(jnp.bfloat16))
        x = x - parts[-1].astype(F32)
    return parts


def joined(a, b, order, axis):
    left = jnp.concatenate([a[i] for i, _ in order], axis=1)
    right = jnp.concatenate([b[j] for _, j in order], axis=axis)
    return lax.dot_general(left, right, (((1,), (axis,)), ((), ())), preferred_element_type=F32)


SIX = ((2, 0), (0, 2), (1, 1), (1, 0), (0, 1), (0, 0))


def nn6(a, b):
    return joined(in_parts(a, 3), in_parts(b, 3), SIX, 0)


def nt6(a, b):
    return joined(in_parts(a, 3), in_parts(b, 3), SIX, 1)


def thrice(a, b):
    return joined(in_parts(a, 2), in_parts(b, 2), ((1, 0), (0, 1), (0, 0)), 0)


def spread(x):
    return jnp.broadcast_to(x, (8, 128))


def tree_sum(terms):
    while len(terms) > 1:
        terms = [terms[i] + terms[i + 1] for i in range(0, len(terms), 2)]
    return terms[0]


def sweep8(cols, sub):
    for a in range(0, 8, 2):
        b = a + 1
        row_a = [spread(c[a : a + 1, :]) for c in cols]
        row_b = [spread(c[b : b + 1, :]) for c in cols]
        aa, ab, bb = row_a[a], row_a[b], row_b[b]
        det = aa * bb - ab * ab
        guess = pl.reciprocal(det, approx=True)
        mend = 2.0 - det * guess
        is_a, is_b = sub == a, sub == b
        part_a = jnp.where(is_a, -bb, jnp.where(is_b, ab, bb * cols[a] - ab * cols[b]))
        part_b = jnp.where(is_a, ab, jnp.where(is_b, -aa, aa * cols[b] - ab * cols[a]))
        new = []
        for j in range(8):
            if j == a:
                new.append(part_a * guess * mend)
            elif j == b:
                new.append(part_b * guess * mend)
            else:
                kept = jnp.where(is_a | is_b, 0.0, cols[j])
                new.append(kept - (part_a * row_a[j] + part_b * row_b[j]) * guess * mend)
        cols = new
    return cols


def sweep(ref):
    lane = lax.broadcasted_iota(jnp.int32, (8, 128), 1)
    sub = lax.broadcasted_iota(jnp.int32, (8, 128), 0)
    rows = [ref[8 * g : 8 * g + 8, :] for g in range(16)]
    for start in (0, 8):
        panel = range(start, start + 8)
        for w in panel:
            k0 = 8 * w
            inside = (lane >= k0) & (lane < k0 + 8)
            pivots = rows[w]
            cols = sweep8([spread(pivots[:, k0 + j : k0 + j + 1]) + 0.0 for j in range(8)], sub)
            terms = []
            for j in range(8):
                row = jnp.where(inside, jnp.where(lane == k0 + j, -1.0, 0.0), spread(pivots[j : j + 1, :]))
                terms.append(cols[j] * row)
            swept = tree_sum(terms)
            minus = [spread(swept[j : j + 1, :]) for j in range(8)]
            for g in list(range(w + 1, start + 8)) + list(range(start, w)):
                terms = [spread(rows[g][:, k0 + j : k0 + j + 1]) * minus[j] for j in range(8)]
                rows[g] = jnp.where(inside, 0.0, rows[g]) + tree_sum(terms)
            rows[w] = -swept
        others = range(8 - start, 16 - start)
        zero = jnp.zeros((8, 128), F32)
        far = jnp.concatenate([rows[g] for g in others], axis=0)
        near = jnp.concatenate([rows[g] if g in panel else zero for g in range(16)], axis=0)
        change = nn(far, near)
        inside = (lane >= 8 * start) & (lane < 8 * start + 64)
        for index, g in enumerate(others):
            rows[g] = jnp.where(inside, 0.0, rows[g]) - change[8 * index : 8 * index + 8, :]
    for g in range(16):
        ref[8 * g : 8 * g + 8, :] = rows[g]


def kernel(
    width, peers, levels,
    jac, damp, rhs, out,
    whole, damp_in, rhs_in, diag, links, half, full, gain, t_out, r_out, c_out, t_in, r_in,
    d_in, d_rhs, map_o, map_n, x_root, x_own, x_o, x_in,
    i_sem, j_send, j_recv, m_send, t_recv, a_recv, p_send, p_recv, d_send, d_recv, token, g_send, g_recv, z_send, x_send, x_recv,
):
    pos = lax.axis_index("tm")
    me = lax.axis_index("rhs")
    middle = width // 2
    tops = list(range(levels - 2, -1, -2))
    core = me % 2

    depth = jac.shape[1]
    mine = pl.ds(pl.multiple_of(me * depth, depth), depth)
    loads = [
        pltpu.make_async_copy(jac, whole.at[:, mine, :], i_sem.at[0]),
        pltpu.make_async_copy(damp, damp_in, i_sem.at[1]),
        pltpu.make_async_copy(rhs, rhs_in, i_sem.at[2]),
    ]
    for load in loads:
        load.start()

    barrier = pltpu.get_barrier_semaphore()
    count = peers - 1
    for d in range(1, peers):
        pl.semaphore_signal(barrier, inc=1, device_id={"rhs": (me + d) % peers}, device_id_type=pl.DeviceIdType.MESH)
    for sign in (-1, 1):
        there = pos + sign
        partner = (there >= 0) & (there < width)
        count = count + partner.astype(jnp.int32)

        @pl.when(partner)
        def _(there=there):
            pl.semaphore_signal(barrier, inc=1, device_id={"tm": there}, device_id_type=pl.DeviceIdType.MESH)
    pl.semaphore_wait(barrier, count)

    def row_copy(k, d):
        return pltpu.make_async_remote_copy(
            src_ref=jac.at[k], dst_ref=whole.at[k, mine, :], send_sem=j_send.at[k, d - 1], recv_sem=j_recv.at[k, d - 1],
            device_id={"rhs": (me + d) % peers}, device_id_type=pl.DeviceIdType.MESH,
        )

    for k in (1, 0):
        for d in range(1, peers):
            row_copy(k, d).start()
    for load in loads:
        load.wait()

    def local_block(k):
        for d in range(1, peers):
            row_copy(k, d).wait()
        on_diag = lax.broadcasted_iota(jnp.int32, (N, N), 0) == lax.broadcasted_iota(jnp.int32, (N, N), 1)
        block = lax.dot_general(whole[k], whole[k], (((0,), (0,)), ((), ())), preferred_element_type=F32)
        extra = damp_in[k : k + 1, :] + (jnp.where(pos > 0, 1.0, 0.0).astype(F32) if k == 0 else 1.0)
        block = block + jnp.where(on_diag, jnp.broadcast_to(extra, (N, N)), 0.0)
        diag[k, 0] = block[:H, :H]
        diag[k, 1] = block[H:, :H]
        diag[k, 2] = block[H:, H:]
        links[k, 2 * N : 2 * N + 8, :] = rhs_in[:, k, :]
        if k == 0:
            links[1, 0:N, :] = -whole[0].astype(F32).T
        else:
            last = jnp.where(pos < width - 1, 1.0, 0.0).astype(F32)
            links[1, N : 2 * N, :] = -whole[1].astype(F32) * last

    local_block(1)

    def coupling_half(slot, which):
        return links.at[0, pl.ds(pl.multiple_of(slot * N + which * H, H), H), :]

    def pair_copy(slot):
        return pltpu.make_async_remote_copy(
            src_ref=coupling_half(slot, core), dst_ref=coupling_half(slot, core), send_sem=p_send.at[slot],
            recv_sem=p_recv.at[slot], device_id={"rhs": me + 1 - 2 * core}, device_id_type=pl.DeviceIdType.MESH,
        )

    def root_copy(part):
        if part < 3:
            src, dst = diag.at[0, part], d_in.at[part]
        else:
            src, dst = links.at[0, 2 * N : 2 * N + 8, :], d_rhs
        return pltpu.make_async_remote_copy(
            src_ref=src, dst_ref=dst, send_sem=d_send.at[part], recv_sem=d_recv.at[part],
            device_id={"tm": middle}, device_id_type=pl.DeviceIdType.MESH,
        )

    def message(t, blk, side, place, hop, part):
        slot = 1 - side
        past = (t == levels - 1) & (pos == middle // 2) & (side == 0)
        at, cell = jnp.where(past, 0, t), jnp.where(past, 1, slot)
        if part < 3:
            src, dst, sem = t_out.at[blk, side, part], t_in.at[at, cell, part], t_recv.at[at, cell, part]
        elif part == 3:
            src, dst, sem = r_out.at[blk, side], r_in.at[at, cell], t_recv.at[at, cell, 3]
        else:
            dst = coupling_half(slot, core)
            src, sem = c_out.at[blk], a_recv.at[slot]
        return pltpu.make_async_remote_copy(
            src_ref=src, dst_ref=dst, send_sem=m_send.at[blk, place, part], recv_sem=sem,
            device_id={"tm": jnp.where(past, middle, pos + hop * (2 * side - 1))}, device_id_type=pl.DeviceIdType.MESH,
        )

    def straight(part):
        dst = t_in.at[0, 1, part] if part < 3 else r_in.at[0, 1]
        return pltpu.make_async_remote_copy(
            src_ref=dst, dst_ref=dst, send_sem=m_send.at[0, 0, part], recv_sem=t_recv.at[0, 1, part],
            device_id={"tm": pos}, device_id_type=pl.DeviceIdType.MESH,
        )

    def exists(there):
        return (there >= 0) & (there < width)

    def next_odd_side(t, step):
        quarter = jnp.where(t == 0, 2 * pos + 1, pos // step) % 4
        return jnp.where(quarter == 1, 1, 0)

    def absorb(t, part):
        def take(slot):
            arrival = message(t - 1, 0, 1 - slot, 0, 1, part)
            arrival.wait_recv()
            if part < 3:
                diag[0, part] = diag[0, part] - t_in[t - 1, slot, part]
            else:
                links[0, 2 * N : 2 * N + 8, :] = links[0, 2 * N : 2 * N + 8, :] - r_in[t - 1, slot]

        @pl.when(pos > 0)
        def _():
            take(0)

        @pl.when(t >= 2)
        def _():
            take(1)

    def products(t, blk, step):
        side_o = next_odd_side(t, step)
        hop = jnp.where(t == 0, 1, step)
        last = t == levels
        y_rows = slice(2 * N, 2 * N + 8)

        def gains(start, size):
            rows = pl.ds(start, size)
            gain[blk, rows, :] = nn(links[blk, rows, :], full[...])

        for place in range(2):
            side = side_o if place == 0 else 1 - side_o
            at = pl.multiple_of(side * N, N)
            other_at = pl.multiple_of((1 - side) * N, N)
            there = pos + hop * (2 * side - 1)
            local = (t == 0) & (side == 0)
            remote = exists(there) & jnp.logical_not(local | last)

            def send(part):
                @pl.when(remote)
                def _():
                    message(t, blk, side, place, hop, part).start()

            def give():
                for part, (r, c) in enumerate(((0, 0), (1, 0), (1, 1))):
                    left = pl.ds(pl.multiple_of(at + r * H, H), H)
                    right = pl.ds(pl.multiple_of(at + c * H, H), H)
                    if part < 2:
                        gains(pl.multiple_of(at + r * H, H), H)
                    t_out[blk, side, part] = nt(gain[blk, left, :], links[blk, right, :])
                    send(part)
                if place == 0:
                    gains(2 * N, 8)
                mat = links[blk, pl.ds(at, N), :]
                r_out[blk, side] = nt(gain[blk, y_rows, :], mat)
                send(3)

                if place == 0:
                    own = pl.ds(pl.multiple_of(other_at + core * H, H), H)
                    gains(pl.multiple_of(other_at + core * H, H), H)
                    c_out[blk] = -nt(gain[blk, own, :], mat)
                    send(4)

                @pl.when(local)
                def _():
                    for part in range(3):
                        diag[0, part] = diag[0, part] - t_out[blk, side, part]
                    links[0, y_rows, :] = links[0, y_rows, :] - r_out[blk, side]
                    if place == 0:
                        gains(other_at, N)
                        links[0, N : 2 * N, :] = -nt(gain[blk, pl.ds(other_at, N), :], mat)

            if place == 0:
                pl.when(jnp.logical_not(last))(give)

                @pl.when(last)
                def _():
                    gains(2 * N, 8)
            else:
                give()

        @pl.when(last)
        def _():
            for part in range(4):
                root_copy(part).wait_recv()
                straight(part).wait_recv()
            for part in range(3):
                diag[0, part] = d_in[part] - t_in[0, 1, part] - t_out[blk, 0, part]
            d_rhs[...] = d_rhs[...] - r_in[0, 1] - r_out[blk, 0]

    def wait_sent(t, blk, step):
        side_o = next_odd_side(t, step)
        hop = jnp.where(t == 0, 1, step)
        for place in range(2):
            side = side_o if place == 0 else 1 - side_o
            there = pos + hop * (2 * side - 1)
            remote = exists(there) & jnp.logical_not(((t == 0) & (side == 0)) | (t == levels))

            @pl.when(remote)
            def _(side=side, place=place):
                for part in range(5 - place):
                    message(t, blk, side, place, hop, part).wait_send()

    def each_map(level, act):
        for sign in (-1, 1) if level > 0 else (-1,):
            there = pos + sign * (2**level // 2 if level > 0 else 1)
            act(
                pltpu.make_async_remote_copy(
                    src_ref=gain.at[0], dst_ref=map_o if level > 0 else map_n,
                    send_sem=g_send.at[0 if sign < 0 else 1], recv_sem=g_recv.at[0 if level > 0 else 1],
                    device_id={"tm": there}, device_id_type=pl.DeviceIdType.MESH,
                )
            )

    def eliminate(t, step):
        blk = jnp.where(t == 0, 1, 0)
        active = (t >= 1) & (t <= levels) & (pos % step == 0) & ((t < levels) | (pos > 0))
        odd = active & (pos // step % 2 == 1)
        root = (t == levels + 1) & (pos == middle)
        invert = (t == 0) | odd | root

        def part_of(h, carry):
            @pl.when((t == 0) & (h == 1))
            def _():
                local_block(0)

            @pl.when(active & (h == 0))
            def _():
                absorb(t, 0)

            @pl.when(active & (h == 0) & (t == levels - 1) & (pos == middle // 2))
            def _():
                pl.semaphore_signal(token, inc=1, device_id={"tm": 0}, device_id_type=pl.DeviceIdType.MESH)

            @pl.when(active & (h == 1))
            def _():
                for part in (1, 2, 3):
                    absorb(t, part)

            @pl.when(invert & (h == 1))
            def _():
                half[...] = -nn6(diag[blk, 1], diag[blk, 0])
                diag[blk, 2] = diag[blk, 2] - nt6(half[...], diag[blk, 1])

            @pl.when(invert)
            def _():
                sweep(diag.at[blk, 2 * h])

            return carry

        lax.fori_loop(0, 2, part_of, 0)

        @pl.when((t == levels - 1) & (pos == 0))
        def _():
            pl.semaphore_wait(token, 1)
            for part in range(4):
                root_copy(part).start()

        def each_coupling(act):
            @pl.when(odd)
            def _():
                act(0)

                @pl.when(t >= 2)
                def _():
                    act(1)

        def hand_on(slot):
            message(t - 1, 0, 1 - slot, 0, 1, 4).wait_recv()
            pair_copy(slot).start()

        each_coupling(hand_on)

        @pl.when(invert)
        def _():
            lower = nn6(diag[blk, 2], half[...])
            upper = lower.T
            full[H:, H:] = -diag[blk, 2]
            full[H:, :H] = lower
            full[:H, H:] = upper
            full[:H, :H] = -diag[blk, 0] - nn6(upper, half[...])

        each_coupling(lambda slot: pair_copy(slot).wait_recv())

        @pl.when(odd | (t == 0))
        def _():
            products(t, blk, step)

        for level in tops:
            @pl.when(odd & (t == level + 1))
            def _(level=level):
                each_map(level, lambda copy: copy.start())

        @pl.when(odd)
        def _():
            wait_sent(t, blk, step)

        each_coupling(lambda slot: pair_copy(slot).wait_send())

        @pl.when(root)
        def _():
            x_root[...] = nn(d_rhs[...], full[...])

        return jnp.where(t == 0, 1, 2 * step)

    lax.fori_loop(0, levels + 2, eliminate, jnp.int32(1))

    def x_copy(src, there, slot, index):
        return pltpu.make_async_remote_copy(
            src_ref=src, dst_ref=x_in.at[slot], send_sem=x_send.at[index], recv_sem=x_recv.at[slot],
            device_id={"tm": there}, device_id_type=pl.DeviceIdType.MESH,
        )

    def wait_for(slot):
        x_copy(x_own, pos, slot, 0).wait_recv()

    def group_targets(at, top):
        if top == 0:
            return [(at + 1, 0), (at - 1, 1), (at - 2, 3)]
        reach = 2**top
        near = [(at + reach, 0), (at - reach, 1)]
        half_reach = reach // 2
        return near + [
            (at + half_reach, 0), (at - half_reach, 1), (at + 3 * half_reach, 2), (at - 3 * half_reach, 2),
        ]

    def each_target(src, at, group_tops, base, act):
        for top in group_tops:
            index = base + 6 * tops.index(top)
            for there, slot in group_targets(at, top):
                @pl.when(exists(there))
                def _(there=there, slot=slot, index=index):
                    act(x_copy(src, there, slot, index))
                index += 1

    def below(level):
        return [top for top in tops if top < level]

    def start(copy):
        copy.start()

    def sent(copy):
        copy.wait_send()

    def take(slot, there):
        @pl.when(there)
        def _():
            wait_for(slot)

        @pl.when(jnp.logical_not(there))
        def _():
            x_in[slot] = jnp.zeros((8, N), F32)

    def solved(of, lower, upper):
        ends = jnp.concatenate([lower, upper], axis=1)
        return of[2 * N : 2 * N + 8, :] - thrice(ends, of[0 : 2 * N, :])

    own_map = gain.at[0]

    def home_copy():
        return pltpu.make_async_remote_copy(
            src_ref=x_root, dst_ref=x_in.at[0], send_sem=z_send, recv_sem=x_recv.at[0],
            device_id={"tm": 0}, device_id_type=pl.DeviceIdType.MESH,
        )

    @pl.when(pos == middle)
    def _():
        each_target(x_root, 0, tops[:1], 0, start)
        x_own[...] = gain[0, 2 * N : 2 * N + 8, :] - thrice(x_root[...], gain[0, 0:N, :])
        each_target(x_own, middle, tops[:1], 24, start)
        each_target(x_root, 0, tops[1:], 0, start)
        each_target(x_own, middle, tops[1:], 24, start)
        home_copy().start()

    @pl.when(pos == 0)
    def _():
        wait_for(0)
        x_own[...] = x_in[0]

    for level in reversed(range(levels - 1)):
        step = 2**level
        top = [t for t in tops if level in (t, t - 1)][0]

        @pl.when(pos % (2 * step) == step)
        def _(level=level, step=step, top=top):
            if level == top:
                take(0, pos >= 0)
                take(1, pos + step < width)
                x_own[...] = solved(own_map, x_in[0], x_in[1])
            else:
                side_o = next_odd_side(1, step)
                side_e = 1 - side_o
                pltpu.make_async_remote_copy(
                    src_ref=own_map, dst_ref=map_o, send_sem=g_send.at[0], recv_sem=g_recv.at[0],
                    device_id={"tm": pos}, device_id_type=pl.DeviceIdType.MESH,
                ).wait_recv()
                take(side_e, exists(pos + step * (2 * side_e - 1)))
                take(2, exists(pos + 3 * step * (2 * side_o - 1)))
                near, far = x_in[side_e], x_in[2]
                flip = side_e == 1
                between = solved(map_o, jnp.where(flip, far, near), jnp.where(flip, near, far))
                x_own[...] = solved(own_map, jnp.where(flip, between, near), jnp.where(flip, near, between))
            if level > 0:
                each_target(x_own, pos, below(level if level == top else top), 0, start)

    out[:, 0, :] = x_own[...]

    @pl.when(pos % 2 == 0)
    def _():
        pltpu.make_async_remote_copy(
            src_ref=own_map, dst_ref=map_n, send_sem=g_send.at[0], recv_sem=g_recv.at[1],
            device_id={"tm": pos}, device_id_type=pl.DeviceIdType.MESH,
        ).wait_recv()
        take(3, pos + 2 < width)
        out[:, 1, :] = solved(gain.at[1], x_own[...], solved(map_n, x_own[...], x_in[3]))

    @pl.when(pos % 2 == 1)
    def _():
        out[:, 1, :] = solved(gain.at[1], x_own[...], x_in[1])

    wait_sent(jnp.int32(0), 1, jnp.int32(1))

    @pl.when(pos == 0)
    def _():
        for part in range(4):
            root_copy(part).wait_send()

    @pl.when(pos == middle)
    def _():
        each_target(x_root, 0, tops, 0, sent)
        each_target(x_own, middle, tops, 24, sent)
        home_copy().wait_send()

    for level in range(levels - 1):
        top = [t for t in tops if level in (t, t - 1)][0]

        @pl.when(pos % (2 * 2**level) == 2**level)
        def _(level=level, top=top):
            if level == top:
                each_map(level, sent)
            if level > 0:
                each_target(x_own, pos, below(level if level == top else top), 0, sent)


def per_device(jacobians, damping, right_sides):
    width = lax.axis_size("tm")
    peers = lax.axis_size("rhs")
    levels = width.bit_length() - 1
    vmem = pl.BlockSpec(memory_space=pltpu.VMEM)
    return pl.pallas_call(
        functools.partial(kernel, width, peers, levels),
        out_shape=jax.ShapeDtypeStruct(right_sides.shape, F32),
        in_specs=[pl.BlockSpec(memory_space=pl.ANY)] * 3,
        out_specs=vmem,
        scratch_shapes=[
            pltpu.VMEM((2, N, N), jnp.bfloat16),
            pltpu.VMEM(damping.shape, F32),
            pltpu.VMEM(right_sides.shape, F32),
            pltpu.VMEM((2, 3, H, H), F32),
            pltpu.VMEM((2, 2 * N + 8, N), F32),
            pltpu.VMEM((H, H), F32),
            pltpu.VMEM((N, N), F32),
            pltpu.VMEM((2, 2 * N + 8, N), F32),
            pltpu.VMEM((2, 2, 3, H, H), F32),
            pltpu.VMEM((2, 2, 8, N), F32),
            pltpu.VMEM((2, H, N), F32),
            pltpu.VMEM((levels, 2, 3, H, H), F32),
            pltpu.VMEM((levels, 2, 8, N), F32),
            pltpu.VMEM((3, H, H), F32),
            pltpu.VMEM((8, N), F32),
            pltpu.VMEM((2 * N + 8, N), F32),
            pltpu.VMEM((2 * N + 8, N), F32),
            pltpu.VMEM((8, N), F32),
            pltpu.VMEM((8, N), F32),
            pltpu.VMEM((8, N), F32),
            pltpu.VMEM((4, 8, N), F32),
            pltpu.SemaphoreType.DMA((3,)),
            pltpu.SemaphoreType.DMA((2, peers - 1)),
            pltpu.SemaphoreType.DMA((2, peers - 1)),
            pltpu.SemaphoreType.DMA((2, 2, 5)),
            pltpu.SemaphoreType.DMA((levels, 2, 4)),
            pltpu.SemaphoreType.DMA((2,)),
            pltpu.SemaphoreType.DMA((2,)),
            pltpu.SemaphoreType.DMA((2,)),
            pltpu.SemaphoreType.DMA((4,)),
            pltpu.SemaphoreType.DMA((4,)),
            pltpu.SemaphoreType.REGULAR,
            pltpu.SemaphoreType.DMA((2,)),
            pltpu.SemaphoreType.DMA((2,)),
            pltpu.SemaphoreType.DMA(()),
            pltpu.SemaphoreType.DMA((48,)),
            pltpu.SemaphoreType.DMA((4,)),
        ],
        compiler_params=pltpu.CompilerParams(
            collective_id=0, has_side_effects=True, vmem_limit_bytes=32 * 1024 * 1024
        ),
    )(jacobians, damping, right_sides)


def solution(mesh):
    in_specs = (P("tm", "rhs", None), P("tm", None), P("rhs", "tm", None))
    return jax.shard_map(
        per_device, mesh=mesh, in_specs=in_specs, out_specs=P("rhs", "tm", None), check_vma=False
    )
```
